256 devices in a mesh: pipe: 4 (over x), mp: 2 (over core), dp: 32 (over y, z).
Axes of the slice: x: 4, y: 4, z: 8, core: 2. Of those that a mesh axis runs over, the one named last changes fastest.
Arguments:
- weights: bfloat16 [4, 2048, 2048], P('pipe', None, 'mp'), may hold values from -1 to 1
- pool: bfloat16 [8192, 2048], P('dp'), may hold values from -24 to 24
- select: int32 [4096], P('dp'), may hold values from 0 to 255
- gradient: float32 [4, 2048, 2048], P('pipe', 'dp', 'mp'), may hold values from -8 to 8
Outputs:
- solution: float32 [4, 2048, 2048], P('pipe', 'dp', 'mp')
- residual: float32 [4, 2048, 2048], P('pipe', 'dp', 'mp')
The draws below stay inside these ranges and needn't reach their ends.
All inputs are finite; a program needn't handle non-finite values.
Results may differ from the reference program's by a relative error of at most 0.039.
Values may be sent and summed in bfloat16 or wider, within the bound.
No kernel may reach another device: no remote copies, remote signals or barrier semaphores. Data moves between devices by JAX's collectives and lax.ppermute only.
A program may use at most 64 MiB of HBM per device.

```python
import math
import jax
import jax.numpy as jnp
import numpy as np
from jax import lax

D = 2048
ROWS_DEV = 128
POOL_DEV = 256
ITERS = 2
LAYERS = 4
ROWS = 4096
POOL = 8192


def column_levels(key, count, low_end, high_end):
    groups = ROWS // ROWS_DEV
    block_width = D // groups
    key_mix, key_rough = jax.random.split(key, 2)
    ramp_pos = jnp.arange(groups, dtype=jnp.float32) / max(groups - 1, 1)
    mixed_pos = 0.5 * ramp_pos[None, :] + 0.5 * jax.random.uniform(key_mix, (count, groups), jnp.float32)
    levels = jnp.exp(math.log(low_end) + (math.log(high_end) - math.log(low_end)) * mixed_pos)
    rough_fac = jnp.exp(jax.random.uniform(key_rough, (count, D), jnp.float32, math.log(0.7), math.log(1.4)))
    return jnp.repeat(levels, block_width, axis=1) * rough_fac


def draw_pool(key, part):
    key_base, key_row, key_col = jax.random.split(jax.random.fold_in(key, 11), 3)
    row_scale = jnp.exp(jax.random.uniform(key_row, (POOL, 1), jnp.float32, math.log(0.3), math.log(3.0)))
    col_scale = column_levels(key_col, 1, 0.1, 4.0)
    base_draw = jnp.clip(jax.random.normal(key_base, (POOL, D), jnp.float32), -4.0, 4.0)
    return jnp.clip(base_draw * row_scale * col_scale, -24.0, 24.0).astype(jnp.bfloat16)


def draw_weights(key, part):
    key_base, key_col = jax.random.split(jax.random.fold_in(key, 23), 2)
    col_scale = column_levels(key_col, LAYERS, 0.1, 3.0)[:, None, :]
    base_draw = jnp.clip(jax.random.normal(key_base, (LAYERS, D, D), jnp.float32), -4.0, 4.0)
    fan_scale = float(D // 2) ** (-0.5)
    return jnp.clip(base_draw * fan_scale * col_scale, -1.0, 1.0).astype(jnp.bfloat16)


def draw_gradient(key, part):
    key_base = jax.random.fold_in(key, 0)
    layer_pos = jnp.arange(LAYERS, dtype=jnp.float32)[:, None, None]
    row_pos = jnp.arange(D, dtype=jnp.float32)[None, :, None]
    ramp_scale = 0.5 * jnp.exp(math.log(3.0) * (layer_pos * D + row_pos) / (LAYERS * D))
    base_draw = jnp.clip(jax.random.normal(key_base, (LAYERS, D, D), jnp.float32), -4.0, 4.0)
    return jnp.clip(base_draw * ramp_scale, -8.0, 8.0)


def plant(array, stream_key, least, high):
    dims = array.shape
    spot = [jax.random.randint(jax.random.fold_in(stream_key, axis), (), 0, dims[axis]) for axis in range(len(dims))]
    array = array.at[tuple(spot)].set(least)
    longest = dims.index(max(dims))
    spot[longest] = (spot[longest] + 1) % dims[longest]
    return array.at[tuple(spot)].set(high)


def cumulative_ranks(count, slope):
    loads = [(1 << 20) // math.isqrt(rank ** slope) + 1 for rank in range(1, count + 1)]
    deviation = 1 + sum(loads) // (1 << 30)
    return np.cumsum(np.array([max(1, weight // deviation) for weight in loads]))


def ranked(own_key, extent, number_of, lean):
    table = cumulative_ranks(number_of, lean)
    lot = jax.random.randint(jax.random.fold_in(own_key, 1), extent, 0, int(table[number_of - 1]))
    rank = jnp.searchsorted(jnp.asarray(table, jnp.int32), lot, side="right")
    return jax.random.permutation(jax.random.fold_in(own_key, 2), number_of)[rank].astype(jnp.int32)


def setup_inputs(seed: int = 0) -> dict:
    seeds = jax.random.split(jax.random.key(seed), 5)
    weights = draw_weights(jax.random.fold_in(seeds[4], 71), 0)
    pool = draw_pool(jax.random.fold_in(seeds[4], 71), 0)
    select = plant(ranked(seeds[2], (ROWS,), POOL_DEV, 2), jax.random.fold_in(seeds[2], 3), 0, POOL_DEV - 1).astype(jnp.int32)
    gradient = draw_gradient(jax.random.fold_in(seeds[4], 71), 0)
    return {"weights": weights, "pool": pool, "select": select, "gradient": gradient}


damping = 0.25


def reference(weights, pool, select, gradient):
    total_rows = select.shape[0]
    owners = jnp.arange(total_rows, dtype=jnp.int32) // ROWS_DEV
    inputs = pool[(owners * POOL_DEV + select).astype(jnp.int32)]
    hidden_list = []
    slope_list = []
    hidden = inputs
    for layer in range(LAYERS):
        pre_act = jnp.dot(hidden, weights[layer], preferred_element_type=jnp.float32)
        tanh_z = jnp.tanh(pre_act)
        hidden_list.append(hidden)
        slope_list.append(1.0 - tanh_z * tanh_z)
        hidden = tanh_z.astype(jnp.bfloat16)

    def product(vector):
        tangent = None
        for layer in range(LAYERS):
            along = jnp.dot(hidden_list[layer], vector[layer].astype(jnp.bfloat16), preferred_element_type=jnp.float32)
            if layer > 0:
                along = jnp.dot(tangent, weights[layer], preferred_element_type=jnp.float32) + along
            tangent = (slope_list[layer] * along).astype(jnp.bfloat16)
        adjoint = tangent
        terms_list = [None] * LAYERS
        for layer in reversed(range(LAYERS)):
            adjoint_pre = (slope_list[layer] * adjoint).astype(jnp.bfloat16)
            terms_list[layer] = lax.dot_general(hidden_list[layer], adjoint_pre, (((0,), (0,)), ((), ())), preferred_element_type=jnp.float32)
            if layer > 0:
                adjoint = lax.dot_general(adjoint_pre, weights[layer], (((1,), (1,)), ((), ())), preferred_element_type=jnp.float32).astype(jnp.bfloat16)
        return jnp.stack(terms_list) / ROWS + damping * vector

    solution = jnp.zeros_like(gradient)
    residual = gradient
    direction = gradient
    norm_now = jnp.sum(residual * residual)
    for step_count in range(ITERS):
        image_vec = product(direction)
        step_len = norm_now / jnp.sum(direction * image_vec)
        solution = solution + step_len * direction
        residual = residual - step_len * image_vec
        norm_next = jnp.sum(residual * residual)
        direction = residual + (norm_next / norm_now) * direction
        norm_now = norm_next
    return solution, residual
```

```python
import jax
import jax.numpy as jnp
from jax import lax
from jax.sharding import Mesh, PartitionSpec as P

damping = 0.25
bf16 = jnp.bfloat16
f32 = jnp.float32


def matmul(left, right):
    return jnp.dot(left, right, preferred_element_type=f32)


def matmul_t(left, right):
    return lax.dot_general(left, right, (((1,), (1,)), ((), ())), preferred_element_type=f32)


def step_pipe(array, by):
    size = lax.axis_size("pipe")
    return lax.ppermute(array, "pipe", [(i, i + by) for i in range(size) if 0 <= i + by < size])


def swap_cores(array):
    return lax.ppermute(array, "mp", [(0, 1), (1, 0)])


def shifts(array, axis):
    size = lax.axis_size(axis)
    return [lax.ppermute(array, axis, [(i, (i + k) % size) for i in range(size)]) for k in range(1, size)]


def ring_sum(array, axis):
    return sum(shifts(array, axis), array)


def local(weights, pool, select, gradient):
    layer_w = weights[0]
    full, half = layer_w.shape
    rows = select.shape[0]
    stages, y_size, z_size = (lax.axis_size(a) for a in ("pipe", "y", "z"))
    total_rows = rows * y_size * z_size
    stage, core = lax.axis_index("pipe"), lax.axis_index("mp")
    grad = gradient[0]
    grad_rows = grad.shape[0]
    thin = half // z_size
    tall = full // y_size

    grad16 = grad.astype(bf16)
    y_at = lax.axis_index("y")
    others = [grad16] + shifts(grad16, "y")
    by_y = jnp.stack(
        [
            lax.select_n((y_at - k) % y_size, *others)
            for k in range(y_size)
        ]
    )
    grad_all = lax.all_gather(by_y, "z", axis=0)
    grad_all = jnp.swapaxes(grad_all, 0, 1).reshape(full, half)

    first = jnp.take(lax.dynamic_slice_in_dim(pool, core * half, half, 1), select, axis=0)
    received = first
    for tick in range(stages):
        incoming = first if tick == 0 else jnp.where(stage == 0, first, received)
        hidden = lax.all_gather(incoming, "mp", axis=1, tiled=True)
        act = jnp.tanh(matmul(hidden, layer_w))
        if tick + 1 < stages:
            received = step_pipe(act.astype(bf16), 1)
    slope = 1.0 - act * act

    hidden_z = lax.all_gather(hidden, "z", axis=0).reshape(z_size * rows, full)

    w_own = lax.dynamic_slice_in_dim(layer_w, core * half, half, 0)
    w_other = lax.dynamic_slice_in_dim(layer_w, (1 - core) * half, half, 0)

    def product(direct):
        tangent = (slope * direct).astype(bf16)
        for tick in range(stages - 1):
            rows_in = lax.all_gather(step_pipe(tangent, 1), "mp", axis=1, tiled=True)
            tangent = (slope * (matmul(rows_in, layer_w) + direct)).astype(bf16)
        incoming = tangent
        for tick in range(stages):
            adjoint = (slope * incoming).astype(bf16)
            if tick + 1 < stages:
                moved = swap_cores(matmul_t(adjoint, w_other).astype(bf16))
                back = (matmul_t(adjoint, w_own) + moved).astype(bf16)
                incoming = jnp.where(stage == stages - 1, tangent, step_pipe(back, -1))
        by_z = jnp.swapaxes(adjoint.reshape(rows, z_size, thin), 0, 1)
        columns = lax.all_to_all(by_z, "z", 0, 0).reshape(z_size * rows, thin)
        partial = lax.dot_general(hidden_z, columns, (((0,), (0,)), ((), ())), preferred_element_type=f32)
        parts = lax.all_to_all(partial.astype(bf16).reshape(y_size, tall, thin), "y", 0, 0)
        tile = jnp.sum(parts.astype(f32), axis=0) / total_rows
        norm = jnp.where(stage == stages - 1, jnp.sum(tangent.astype(f32) ** 2), 0.0) / total_rows
        return tile, norm

    u_tile, gu = product(matmul(hidden, grad_all))
    u16 = u_tile.astype(bf16)
    uu = jnp.sum(u16.astype(f32) ** 2)
    u_cols = lax.all_to_all(jnp.broadcast_to(u16, (y_size, tall, thin)), "y", 0, 0).reshape(full, thin)
    along = matmul(hidden_z, u_cols).astype(bf16).reshape(z_size, rows, thin)
    along = lax.all_to_all(along, "z", 0, 0)
    along = jnp.swapaxes(along, 0, 1).reshape(rows, half).astype(f32)
    w_tile, uw = product(along)

    sums = jnp.stack([jnp.sum(grad * grad), gu, uu, uw])
    sums = jnp.broadcast_to(sums[:, None], (4, 128))
    for axis in ("mp", "pipe", "y"):
        sums = ring_sum(sums, axis)
    sums = lax.all_to_all(jnp.broadcast_to(sums, (z_size, 4, 128)), "z", 0, 0)
    rr0, gu, uu, uw = jnp.sum(sums, axis=0)[:, 0]

    both = jnp.stack([u16, w_tile.astype(bf16)]).reshape(2, z_size, grad_rows, thin)
    both = lax.all_to_all(both, "z", 1, 1)
    both = jnp.swapaxes(both, 1, 2).reshape(2, grad_rows, half).astype(f32)
    u, w = both[0], both[1]

    scale = gu + damping * rr0
    len0 = rr0 / scale
    keep = gu / scale
    rr1 = len0 * len0 * (uu - gu * gu / rr0)
    c1 = keep + rr1 / rr0
    c2 = -len0
    d_d = c1 * c1 * rr0 + 2.0 * c1 * c2 * gu + c2 * c2 * uu
    d_image = c1 * c1 * gu + 2.0 * c1 * c2 * uu + c2 * c2 * uw + damping * d_d
    len1 = rr1 / d_image
    direction = c1 * grad + c2 * u
    image = c1 * u + c2 * w + damping * direction
    solved = len0 * grad + len1 * direction
    residual = keep * grad - len0 * u - len1 * image
    return solved[None], residual[None]


def solution(mesh):
    pipe, mp, _ = mesh.devices.shape
    fine = Mesh(mesh.devices.reshape(pipe, mp, 4, 8), ("pipe", "mp", "y", "z"))
    dp = ("y", "z")
    return jax.shard_map(
        local,
        mesh=fine,
        in_specs=(P("pipe", None, "mp"), P(dp, None), P(dp), P("pipe", dp, "mp")),
        out_specs=(P("pipe", dp, "mp"), P("pipe", dp, "mp")),
        check_vma=False,
    )
```

```python
import jax
import jax.numpy as jnp
from jax import lax
from jax.sharding import Mesh, PartitionSpec as P

damping = 0.25
bf16 = jnp.bfloat16
f32 = jnp.float32
pipe = ("pp", "pr")
team = ("pr", "mp")
wide = ("pr", "mp", "z")


def matmul(left, right):
    return jnp.dot(left, right, preferred_element_type=f32)


def matmul_t(left, right):
    return lax.dot_general(left, right, (((1,), (1,)), ((), ())), preferred_element_type=f32)


def swap(array, axis):
    return lax.ppermute(array, axis, [(0, 1), (1, 0)])


def shifts(array, axis):
    size = lax.axis_size(axis)
    return [lax.ppermute(array, axis, [(i, (i + k) % size) for i in range(size)]) for k in range(1, size)]


def ring_sum(array, axis):
    return sum(shifts(array, axis), array)


def local(weights, pool, select, gradient):
    layer_w = weights[0]
    full, half = layer_w.shape
    rows = select.shape[0]
    stages = lax.axis_size(pipe)
    y_size, z_size = lax.axis_size("y"), lax.axis_size("z")
    total_rows = rows * y_size * z_size
    pair, place, core = (lax.axis_index(a) for a in ("pp", "pr", "mp"))
    y_at = lax.axis_index("y")
    stage = 2 * pair + place
    grad = gradient[0]
    grad_rows = grad.shape[0]
    thin = half // z_size
    tall = full // y_size
    members = 4
    mine = rows // members

    grad16 = grad.astype(bf16)
    others = [grad16] + shifts(grad16, "y")
    by_y = jnp.stack([lax.select_n((y_at - k) % y_size, *others) for k in range(y_size)])
    grad_all = lax.all_gather(by_y, "z", axis=0)
    grad_all = jnp.swapaxes(grad_all, 0, 1).reshape(full, half)

    share = 3 * full // 16
    straight = full - y_size * share
    sent = lax.dynamic_slice_in_dim(layer_w, straight + y_at * share, share, 0)
    got = swap(sent, "pr")
    got = [got] + shifts(got, "y")
    mate_w = jnp.concatenate([swap(layer_w[:straight], "pr"), jnp.zeros((y_size * share, half), bf16)])
    for k in range(y_size):
        mate_w = lax.dynamic_update_slice_in_dim(mate_w, got[k], straight + (y_at - k) % y_size * share, 0)
    halves = [[layer_w, swap(layer_w, "mp")], [mate_w, swap(mate_w, "mp")]]

    first = jnp.take(lax.dynamic_slice_in_dim(pool, core * half, half, 1), select, axis=0)
    received = first
    for tick in range(stages):
        incoming = first if tick == 0 else jnp.where(stage == 0, first, received)
        hidden = lax.all_gather(incoming, "mp", axis=1, tiled=True)
        act = jnp.tanh(matmul(hidden, layer_w))
        if tick + 1 < stages:
            received = lax.ppermute(act.astype(bf16), pipe, [(i, i + 1) for i in range(stages - 1)])
    slope = 1.0 - act * act

    def in_order(array):
        return jnp.where(pair == 1, jnp.roll(array, rows // 2, axis=0), array)

    hidden = in_order(hidden)

    def to_team(array):
        parts = lax.all_to_all(array.reshape(members, mine, half), team, 0, 0)
        parts = jnp.swapaxes(parts.reshape(2, 2, mine, half), 1, 2)
        return parts.reshape(2, mine, full)

    slopes = to_team(in_order(slope))

    hidden_z = lax.all_gather(hidden, "z", axis=0).reshape(z_size, members, mine, full)
    hidden_z = jnp.swapaxes(hidden_z, 0, 1).reshape(z_size * rows, full)

    def on_layers(work, *arrays):
        def branch(place_at, core_at):
            def run(held, *given):
                pair_w = [held[i][::-1] if core_at else held[i] for i in (place_at, 1 - place_at)]
                return work(*pair_w, *given)

            return run

        return lax.switch(2 * place + core, [branch(i, j) for i in (0, 1) for j in (0, 1)], halves, *arrays)

    def ahead(array, layer):
        return jnp.concatenate([matmul(array, part) for part in layer], axis=1)

    def back(array, layer):
        return sum(matmul_t(array[:, i * half : (i + 1) * half], layer[i]) for i in (0, 1)).astype(bf16)

    def product(direct):
        t_0 = (slopes[0] * direct[0]).astype(bf16)

        def start(w_0, w_1, t_0, slope_1, direct_1):
            return (slope_1 * (ahead(t_0, w_1) + direct_1)).astype(bf16)

        t_1 = on_layers(start, t_0, slopes[1], direct[1])
        received = lax.ppermute(t_1, pipe, [(0, 3), (1, 2)])

        def turn(w_0, w_1, received, slopes, direct):
            t_0 = (slopes[0] * (ahead(received, w_0) + direct[0])).astype(bf16)
            t_1 = (slopes[1] * (ahead(t_0, w_1) + direct[1])).astype(bf16)
            g_1 = (slopes[1] * t_1).astype(bf16)
            g_0 = (slopes[0] * back(g_1, w_1)).astype(bf16)
            return t_1, back(g_0, w_0)

        t_1, e_0 = on_layers(turn, received, slopes, direct)
        received = lax.ppermute(e_0, pipe, [(3, 0), (2, 1)])
        g_1 = (slopes[1] * jnp.where(pair == 1, t_1, received)).astype(bf16)

        def finish(w_0, w_1, g_1, slope_0):
            return (slope_0 * back(g_1, w_1)).astype(bf16)

        g_0 = on_layers(finish, g_1, slopes[0])
        g = jnp.stack([g_0, g_1]).reshape(2, mine, 2 * z_size, thin)
        g = jnp.swapaxes(g, 1, 2).reshape(members * z_size, mine, thin)
        columns = lax.all_to_all(g, wide, 0, 0).reshape(z_size * rows, thin)
        partial = lax.dot_general(hidden_z, columns, (((0,), (0,)), ((), ())), preferred_element_type=f32)
        parts = lax.all_to_all(partial.astype(bf16).reshape(y_size, tall, thin), "y", 0, 0)
        tile = jnp.sum(parts.astype(f32), axis=0) / total_rows
        norm = jnp.where(pair == 1, jnp.sum(t_1.astype(f32) ** 2), 0.0) / total_rows
        return tile, norm

    u_tile, gu = product(to_team(matmul(hidden, grad_all).astype(bf16)).astype(f32))
    u16 = u_tile.astype(bf16)
    uu = jnp.sum(u16.astype(f32) ** 2)
    u_cols = lax.all_to_all(jnp.broadcast_to(u16, (y_size, tall, thin)), "y", 0, 0).reshape(full, thin)
    along = matmul(hidden_z, u_cols).astype(bf16).reshape(members * z_size, mine, thin)
    along = lax.all_to_all(along, wide, 0, 0).reshape(2, 2 * z_size, mine, thin)
    along = jnp.swapaxes(along, 1, 2).reshape(2, mine, full).astype(f32)
    w_tile, uw = product(along)

    sums = jnp.stack([jnp.sum(grad * grad), gu, uu, uw])
    sums = jnp.broadcast_to(sums[:, None], (4, 128))
    for axis in ("mp", "pr", "pp", "y"):
        sums = ring_sum(sums, axis)
    sums = lax.all_to_all(jnp.broadcast_to(sums, (z_size, 4, 128)), "z", 0, 0)
    rr0, gu, uu, uw = jnp.sum(sums, axis=0)[:, 0]

    both = jnp.stack([u16, w_tile.astype(bf16)]).reshape(2, z_size, grad_rows, thin)
    both = lax.all_to_all(both, "z", 1, 1)
    both = jnp.swapaxes(both, 1, 2).reshape(2, grad_rows, half).astype(f32)
    u, w = both[0], both[1]

    scale = gu + damping * rr0
    len0 = rr0 / scale
    keep = gu / scale
    rr1 = len0 * len0 * (uu - gu * gu / rr0)
    c1 = keep + rr1 / rr0
    c2 = -len0
    d_d = c1 * c1 * rr0 + 2.0 * c1 * c2 * gu + c2 * c2 * uu
    d_image = c1 * c1 * gu + 2.0 * c1 * c2 * uu + c2 * c2 * uw + damping * d_d
    len1 = rr1 / d_image
    direction = c1 * grad + c2 * u
    image = c1 * u + c2 * w + damping * direction
    solved = len0 * grad + len1 * direction
    residual = keep * grad - len0 * u - len1 * image
    return solved[None], residual[None]


def solution(mesh):
    fine = Mesh(mesh.devices.reshape(2, 2, 2, 4, 8), ("pp", "pr", "mp", "y", "z"))
    dp = ("y", "z")
    return jax.shard_map(
        local,
        mesh=fine,
        in_specs=(P(pipe, None, "mp"), P(dp, None), P(dp), P(pipe, dp, "mp")),
        out_specs=(P(pipe, dp, "mp"), P(pipe, dp, "mp")),
        check_vma=False,
    )
```

```python
import functools

import jax
import jax.numpy as jnp
from jax import lax
from jax.experimental import pallas as pl
from jax.experimental.pallas import tpu as pltpu
from jax.sharding import Mesh, PartitionSpec as P

damping = 0.25
bf16 = jnp.bfloat16
f32 = jnp.float32
pipe = ("pp", "pr")
team = ("pr", "mp")
wide = ("pr", "mp", "z")


def matmul(left, right):
    return jnp.dot(left, right, preferred_element_type=f32)


def matmul_t(left, right):
    return lax.dot_general(left, right, (((1,), (1,)), ((), ())), preferred_element_type=f32)


def swap(array, axis):
    return lax.ppermute(array, axis, [(0, 1), (1, 0)])


def shift(array, axis, by):
    size = lax.axis_size(axis)
    return lax.ppermute(array, axis, [(i, (i + by) % size) for i in range(size)])


def shifts(array, axis):
    return [shift(array, axis, k) for k in range(1, lax.axis_size(axis))]


def back(array, w_ref, layer):
    half = w_ref.shape[3]
    return sum(matmul_t(array[:, i * half : (i + 1) * half], w_ref[layer, i]) for i in (0, 1)).astype(bf16)


def pass_layer(array, w_ref, layer, slope_ref, direct_ref, out_ref):
    half = w_ref.shape[3]
    for i in (0, 1):
        at = pl.ds(i * half, half)
        made = matmul(array, w_ref[layer, i]) + direct_ref[layer, :, at].astype(f32)
        out_ref[:, at] = (slope_ref[layer, :, at].astype(f32) * made).astype(bf16)


def start_body(w_ref, slope_ref, direct_ref, t_ref, scratch):
    scratch[...] = (slope_ref[0].astype(f32) * direct_ref[0].astype(f32)).astype(bf16)
    pass_layer(scratch[...], w_ref, 1, slope_ref, direct_ref, t_ref)


def turn_body(w_ref, slope_ref, direct_ref, received_ref, t_ref, e_ref, norm_ref, scratch):
    pass_layer(received_ref[...], w_ref, 0, slope_ref, direct_ref, scratch)
    pass_layer(scratch[...], w_ref, 1, slope_ref, direct_ref, t_ref)
    t_1 = t_ref[...].astype(f32)
    norm_ref[...] = jnp.broadcast_to(jnp.sum(t_1 * t_1, axis=(0, 1), keepdims=True), norm_ref.shape)
    g_1 = (slope_ref[1].astype(f32) * t_1).astype(bf16)
    g_0 = (slope_ref[0].astype(f32) * back(g_1, w_ref, 1).astype(f32)).astype(bf16)
    e_ref[...] = back(g_0, w_ref, 0)


def finish_body(w_ref, slope_ref, e_ref, g_ref):
    g_1 = (slope_ref[1].astype(f32) * e_ref[...].astype(f32)).astype(bf16)
    g_ref[1] = g_1
    g_ref[0] = (slope_ref[0].astype(f32) * back(g_1, w_ref, 1).astype(f32)).astype(bf16)


def collect_body(at_ref, *refs):
    parts, (w_ref, sems) = refs[:-2], refs[-2:]
    place, core, y_at = at_ref[0], at_ref[1], at_ref[2]
    count = len(parts) // 2
    share = parts[1].shape[0]
    y_size = w_ref.shape[2] // share
    copies = []
    for i, part in enumerate(parts):
        k, column = i % count, core if i < count else 1 - core
        if k == 0:
            target = w_ref.at[place, column]
        else:
            row = (y_at + (0, y_size - 1, 1, 2, 2)[k - 1]) % y_size * share + (share // 2 if k == 5 else 0)
            target = w_ref.at[1 - place, column, pl.ds(pl.multiple_of(row, 16), part.shape[0])]
        copies.append(pltpu.make_async_copy(part, target, sems.at[i]))
    for copy in copies:
        copy.start()
    for copy in copies:
        copy.wait()


vmem = pl.BlockSpec(memory_space=pltpu.VMEM)
params = pltpu.CompilerParams(vmem_limit_bytes=24 << 20)


def local(weights, pool, select, gradient):
    layer_w = weights[0]
    full, half = layer_w.shape
    rows = select.shape[0]
    stages = lax.axis_size(pipe)
    y_size, z_size = lax.axis_size("y"), lax.axis_size("z")
    total_rows = rows * y_size * z_size
    pair, place, core = (lax.axis_index(a) for a in ("pp", "pr", "mp"))
    y_at = lax.axis_index("y")
    stage = 2 * pair + place
    grad = gradient[0]
    grad_rows = grad.shape[0]
    thin = half // z_size
    tall = full // y_size
    members = 4
    mine = rows // members

    share = full // y_size
    grad16, rr0 = grad.astype(bf16), jnp.sum(grad * grad)
    sent = lax.dynamic_slice_in_dim(layer_w, y_at * share, share, 0)
    grad16, sent, rr0 = lax.optimization_barrier((grad16, sent, rr0))
    own_share = swap(sent, "pr")
    others = [grad16] + shifts(grad16, "y")
    by_y = jnp.stack([lax.select_n((y_at - k) % y_size, *others) for k in range(y_size)])
    grad_all = lax.all_gather(by_y, "z", axis=0).reshape(full, half)
    own_x = swap(layer_w, "mp")

    first = jnp.take(lax.dynamic_slice_in_dim(pool, core * half, half, 1), select, axis=0)
    first, own_x, own_share = lax.optimization_barrier((first, own_x, own_share))
    received, shares = first, [own_share, shift(own_share, "y", 1), shift(own_share, "y", -1)]
    shares_x = [swap(own_share, "mp")]
    for tick in range(stages):
        if tick == 2:
            received, shares, shares_x = lax.optimization_barrier((received, shares, shares_x))
            shares += [shift(shares[1][: share // 2], "y", 1), shift(shares[2][share // 2 :], "y", -1)]
            shares_x += [swap(part, "mp") for part in shares[1:3]]
        if tick == 3:
            received, shares, shares_x = lax.optimization_barrier((received, shares, shares_x))
            shares_x += [swap(part, "mp") for part in shares[3:]]
        incoming = first if tick == 0 else jnp.where(stage == 0, first, received)
        hidden = lax.all_gather(incoming, "mp", axis=1, tiled=True)
        act = jnp.tanh(matmul(hidden, layer_w))
        if tick + 1 < stages:
            received = lax.ppermute(act.astype(bf16), pipe, [(i, i + 1) for i in range(stages - 1)])
    slope = 1.0 - act * act

    def in_order(array):
        return jnp.where(pair == 1, jnp.roll(array, rows // 2, axis=0), array)

    hidden = in_order(hidden)
    by_row = hidden.reshape(rows, y_size, z_size, grad_rows)
    by_row = lax.optimization_barrier(jnp.swapaxes(by_row, 1, 2).reshape(rows, full))

    hidden_z = lax.all_gather(hidden, "z", axis=0).reshape(z_size * rows, full)

    given = jnp.stack([in_order(slope).astype(bf16), matmul(by_row, grad_all).astype(bf16)])
    given = jnp.swapaxes(given.reshape(2, members, mine, half), 0, 1)
    parts = [layer_w, *shares, own_x, *shares_x]
    parts, given = lax.optimization_barrier((parts, given))
    parts = [pltpu.with_memory_space_constraint(part, pltpu.HBM) for part in parts]
    held = pl.pallas_call(
        collect_body,
        out_shape=pltpu.VMEM((2, 2, full, half), bf16),
        in_specs=[pl.BlockSpec(memory_space=pltpu.SMEM)] + [pl.BlockSpec(memory_space=pltpu.HBM)] * len(parts),
        out_specs=vmem,
        scratch_shapes=[pltpu.SemaphoreType.DMA((len(parts),))],
        compiler_params=params,
        name="collect",
    )(jnp.stack([place, core, y_at]), *parts)

    given, held = lax.optimization_barrier((given, held))
    given = lax.all_to_all(given, team, 0, 0).reshape(2, 2, 2, mine, half)
    slopes, direct_g = (jnp.swapaxes(given[:, :, i], 1, 2).reshape(2, mine, full) for i in (0, 1))

    block = jax.ShapeDtypeStruct((mine, full), bf16)
    tile_of_f32 = jax.ShapeDtypeStruct((8, 128), f32)
    two = jax.ShapeDtypeStruct((2, mine, full), bf16)

    def on_layers(body, out_shape, *arrays, scratch=()):
        return pl.pallas_call(
            body,
            out_shape=out_shape,
            in_specs=[vmem] * (1 + len(arrays)),
            out_specs=jax.tree.map(lambda _: vmem, out_shape),
            scratch_shapes=list(scratch),
            compiler_params=params,
            name=body.__name__,
        )(held, *arrays)

    def product(direct, sums=None):
        room = [pltpu.VMEM((mine, full), bf16)]
        t_1 = on_layers(start_body, block, slopes, direct, scratch=room)
        received = lax.ppermute(t_1, pipe, [(0, 3), (1, 2)])
        t_1, e_0, norm = on_layers(turn_body, (block, block, tile_of_f32), slopes, direct, received, scratch=room)
        received = lax.ppermute(e_0, pipe, [(3, 0), (2, 1)])
        g = on_layers(finish_body, two, slopes, jnp.where(pair == 1, t_1, received))
        norm = jnp.where(pair == 1, norm[:1], 0.0) / total_rows
        g = jnp.swapaxes(g.reshape(2, mine, 2 * z_size, thin), 1, 2)
        g = g.reshape(members * z_size, mine, thin)
        if sums is not None:
            g = ride(g, jnp.concatenate([sums, norm]))
        g = lax.all_to_all(g, wide, 0, 0)
        columns = jnp.swapaxes(g[:, :mine].reshape(members, z_size, mine, thin), 0, 1).reshape(z_size * rows, thin)
        parts = lax.dot_general(hidden_z, columns, (((0,), (0,)), ((), ())), preferred_element_type=f32).astype(bf16).reshape(y_size, tall, thin)
        if sums is not None:
            parts = ride(parts, alight(g, mine))
        parts = lax.all_to_all(parts, "y", 0, 0)
        if sums is not None:
            norm = alight(parts, tall)
        tile = jnp.sum(parts[:, :tall].astype(f32), axis=0) / total_rows
        return tile, norm

    def ride(array, sums):
        parts = []
        for _ in range(3):
            parts.append(lax.reduce_precision(sums, 8, 7))
            sums = sums - parts[-1]
        parts = jnp.concatenate(parts + [jnp.zeros_like(sums)]).astype(bf16)
        return jnp.concatenate([array, jnp.broadcast_to(parts, (array.shape[0], *parts.shape))], axis=1)

    def alight(array, from_row):
        return jnp.sum(array[:, from_row : from_row + 12].astype(f32).reshape(-1, 4, thin), axis=0)

    u_tile, gu = product(direct_g)
    u16 = u_tile.astype(bf16)
    uu = jnp.sum(u16.astype(f32) ** 2)
    u_cols = lax.all_to_all(jnp.broadcast_to(u16, (y_size, tall, thin)), "y", 0, 0).reshape(full, thin)
    along = matmul(hidden_z, u_cols).astype(bf16).reshape(z_size, members, mine, thin)
    along = jnp.swapaxes(along, 0, 1).reshape(members * z_size, mine, thin)
    sums = jnp.concatenate([jnp.full((1, thin), rr0), gu, jnp.full((1, thin), uu)])
    along, sums = lax.optimization_barrier((along, sums))
    along = lax.all_to_all(along, wide, 0, 0).reshape(2, 2 * z_size, mine, thin)
    along = jnp.swapaxes(along, 1, 2).reshape(2, mine, full)
    w_tile, sums = product(along, sums)
    rr0, gu, uu, uw = (sums + swap(sums, "pp"))[:, 0]

    both = jnp.stack([u16, w_tile.astype(bf16)]).reshape(2, z_size, grad_rows, thin)
    both = lax.all_to_all(both, "z", 1, 1)
    both = jnp.swapaxes(both, 1, 2).reshape(2, grad_rows, half).astype(f32)
    u, w = both[0], both[1]

    scale = gu + damping * rr0
    len0 = rr0 / scale
    keep = gu / scale
    rr1 = len0 * len0 * (uu - gu * gu / rr0)
    c1 = keep + rr1 / rr0
    c2 = -len0
    d_d = c1 * c1 * rr0 + 2.0 * c1 * c2 * gu + c2 * c2 * uu
    d_image = c1 * c1 * gu + 2.0 * c1 * c2 * uu + c2 * c2 * uw + damping * d_d
    len1 = rr1 / d_image
    direction = c1 * grad + c2 * u
    image = c1 * u + c2 * w + damping * direction
    solved = len0 * grad + len1 * direction
    residual = keep * grad - len0 * u - len1 * image
    return solved[None], residual[None]


def solution(mesh):
    fine = Mesh(mesh.devices.reshape(2, 2, 2, 4, 8), ("pp", "pr", "mp", "y", "z"))
    dp = ("y", "z")
    return jax.shard_map(
        local,
        mesh=fine,
        in_specs=(P(pipe, None, "mp"), P(dp, None), P(dp), P(pipe, dp, "mp")),
        out_specs=(P(pipe, dp, "mp"), P(pipe, dp, "mp")),
        check_vma=False,
    )
```

```python
import functools

import jax
import jax.numpy as jnp
from jax import lax
from jax.experimental import pallas as pl
from jax.experimental.pallas import tpu as pltpu
from jax.sharding import Mesh, PartitionSpec as P

damping = 0.25
bf16 = jnp.bfloat16
f32 = jnp.float32
pipe = ("pp", "pr")
team = ("pr", "mp")
wide = ("pr", "mp", "z")


def matmul(left, right):
    return jnp.dot(left, right, preferred_element_type=f32)


def matmul_t(left, right):
    return lax.dot_general(left, right, (((1,), (1,)), ((), ())), preferred_element_type=f32)


def swap(array, axis):
    return lax.ppermute(array, axis, [(0, 1), (1, 0)])


def shift(array, axis, by):
    size = lax.axis_size(axis)
    return lax.ppermute(array, axis, [(i, (i + by) % size) for i in range(size)])


def shifts(array, axis):
    return [shift(array, axis, k) for k in range(1, lax.axis_size(axis))]


def back(array, w_ref, layer):
    half = w_ref.shape[3]
    return sum(matmul_t(array[:, i * half : (i + 1) * half], w_ref[layer, i]) for i in (0, 1)).astype(bf16)


def pass_layer(array, w_ref, layer, slope_ref, direct_ref, out_ref):
    half = w_ref.shape[3]
    for i in (0, 1):
        at = pl.ds(i * half, half)
        made = matmul(array, w_ref[layer, i]) + direct_ref[layer, :, at].astype(f32)
        out_ref[:, at] = (slope_ref[layer, :, at].astype(f32) * made).astype(bf16)


def start_body(w_ref, slope_ref, direct_ref, t_ref, scratch):
    scratch[...] = (slope_ref[0].astype(f32) * direct_ref[0].astype(f32)).astype(bf16)
    pass_layer(scratch[...], w_ref, 1, slope_ref, direct_ref, t_ref)


def turn_body(w_ref, slope_ref, direct_ref, received_ref, t_ref, e_ref, norm_ref, scratch):
    pass_layer(received_ref[...], w_ref, 0, slope_ref, direct_ref, scratch)
    pass_layer(scratch[...], w_ref, 1, slope_ref, direct_ref, t_ref)
    t_1 = t_ref[...].astype(f32)
    norm_ref[...] = jnp.broadcast_to(jnp.sum(t_1 * t_1, axis=(0, 1), keepdims=True), norm_ref.shape)
    g_1 = (slope_ref[1].astype(f32) * t_1).astype(bf16)
    g_0 = (slope_ref[0].astype(f32) * back(g_1, w_ref, 1).astype(f32)).astype(bf16)
    e_ref[...] = back(g_0, w_ref, 0)


def finish_body(w_ref, slope_ref, e_ref, g_ref):
    g_1 = (slope_ref[1].astype(f32) * e_ref[...].astype(f32)).astype(bf16)
    g_ref[1] = g_1
    g_ref[0] = (slope_ref[0].astype(f32) * back(g_1, w_ref, 1).astype(f32)).astype(bf16)


def collect_body(at_ref, *refs):
    parts, (w_ref, sems) = refs[:-2], refs[-2:]
    place, core, y_at = at_ref[0], at_ref[1], at_ref[2]
    count = len(parts) // 2
    chunk = parts[1].shape[0]
    y_size = w_ref.shape[2] // chunk // 2
    copies = []
    for i, part in enumerate(parts):
        k, column = i % count, core if i < count else 1 - core
        if k == 0:
            target = w_ref.at[place, column]
        else:
            owner = (y_at + (0, y_size - 1, 1, 2)[(k - 1) // 2]) % y_size
            row = pl.multiple_of((2 * owner + (k - 1) % 2) * chunk, 16)
            target = w_ref.at[1 - place, column, pl.ds(row, chunk)]
        copies.append(pltpu.make_async_copy(part, target, sems.at[i]))
    for copy in copies:
        copy.start()
    for copy in copies:
        copy.wait()


def update_body(sums_ref, other_ref, both_ref, grad_ref, solved_ref, residual_ref):
    thin = sums_ref.shape[1]
    rows = sums_ref[...] + other_ref[...]
    rr0, gu, uu, uw = (rows[i : i + 1] for i in range(4))
    scale = gu + damping * rr0
    len0 = rr0 / scale
    keep = gu / scale
    rr1 = len0 * len0 * (uu - gu * gu / rr0)
    c1 = keep + rr1 / rr0
    c2 = -len0
    d_d = c1 * c1 * rr0 + 2.0 * c1 * c2 * gu + c2 * c2 * uu
    d_image = c1 * c1 * gu + 2.0 * c1 * c2 * uu + c2 * c2 * uw + damping * d_d
    len1 = rr1 / d_image
    for k in range(both_ref.shape[1]):
        at = pl.ds(k * thin, thin)
        g, u, w = grad_ref[:, at], both_ref[0, k].astype(f32), both_ref[1, k].astype(f32)
        direction = c1 * g + c2 * u
        image = c1 * u + c2 * w + damping * direction
        solved_ref[:, at] = len0 * g + len1 * direction
        residual_ref[:, at] = keep * g - len0 * u - len1 * image


vmem = pl.BlockSpec(memory_space=pltpu.VMEM)
params = pltpu.CompilerParams(vmem_limit_bytes=24 << 20)


def local(weights, pool, select, gradient):
    layer_w = weights[0]
    full, half = layer_w.shape
    rows = select.shape[0]
    stages = lax.axis_size(pipe)
    y_size, z_size = lax.axis_size("y"), lax.axis_size("z")
    total_rows = rows * y_size * z_size
    pair, place, core = (lax.axis_index(a) for a in ("pp", "pr", "mp"))
    y_at = lax.axis_index("y")
    stage = 2 * pair + place
    grad = gradient[0]
    grad_rows = grad.shape[0]
    thin = half // z_size
    tall = full // y_size
    members = 4
    mine = rows // members

    chunk = full // y_size // 2
    grad16 = grad.astype(bf16)
    sent = [lax.dynamic_slice_in_dim(layer_w, (2 * y_at + i) * chunk, chunk, 0) for i in (0, 1)]
    grad16, sent[0] = lax.optimization_barrier((grad16, sent[0]))
    a_0, b_0 = (swap(part, "pr") for part in sent)
    own_x = swap(layer_w, "mp")
    others, a_0 = lax.optimization_barrier((shifts(grad16, "y"), a_0))
    others = [grad16] + others
    by_y = jnp.stack([lax.select_n((y_at - k) % y_size, *others) for k in range(y_size)])
    grad_all = lax.all_gather(by_y, "z", axis=0).reshape(full, half)

    first = jnp.take(lax.dynamic_slice_in_dim(pool, core * half, half, 1), select, axis=0)
    first, own_x = lax.optimization_barrier((first, own_x))
    received = first
    for tick in range(stages):
        if tick == 0:
            a_p, a_m = shift(a_0, "y", 1), shift(a_0, "y", -1)
        if tick == 1:
            received, a_p, a_m = lax.optimization_barrier((received, a_p, a_m))
            a_2, b_p, b_m = shift(a_p, "y", 1), shift(b_0, "y", 1), shift(b_0, "y", -1)
            crossed = [swap(part, "mp") for part in (a_0, b_0)]
        if tick == 2:
            received, b_m, crossed, late = lax.optimization_barrier((received, b_m, crossed, grad))
            b_2, rr0 = shift(b_m, "y", -1), jnp.sum(late * late)
            crossed += [swap(part, "mp") for part in (a_p, a_m)]
        if tick == 3:
            received, a_2, b_2, b_p, crossed, rr0 = lax.optimization_barrier((received, a_2, b_2, b_p, crossed, rr0))
            crossed += [swap(part, "mp") for part in (b_p, b_m, a_2, b_2)]
        incoming = first if tick == 0 else jnp.where(stage == 0, first, received)
        hidden = lax.all_gather(incoming, "mp", axis=1, tiled=True)
        act = jnp.tanh(matmul(hidden, layer_w))
        if tick == 0:
            act, b_0 = lax.optimization_barrier((act, b_0))
        if tick + 1 < stages:
            received = lax.ppermute(act.astype(bf16), pipe, [(i, i + 1) for i in range(stages - 1)])
    slope = 1.0 - act * act

    def in_order(array):
        return jnp.where(pair == 1, jnp.roll(array, rows // 2, axis=0), array)

    hidden = in_order(hidden)
    by_row = hidden.reshape(rows, y_size, z_size, grad_rows)
    by_row = lax.optimization_barrier(jnp.swapaxes(by_row, 1, 2).reshape(rows, full))

    hidden_z = lax.all_gather(hidden, "z", axis=0).reshape(z_size * rows, full)

    given = jnp.stack([in_order(slope).astype(bf16), matmul(by_row, grad_all).astype(bf16)])
    given = jnp.swapaxes(given.reshape(2, members, mine, half), 0, 1)
    parts = [layer_w, a_0, b_0, a_p, b_p, a_m, b_m, a_2, b_2, own_x, *(crossed[i] for i in (0, 1, 2, 4, 3, 5, 6, 7))]
    parts, given = lax.optimization_barrier((parts, given))
    at = 2 * place + core

    def from_mate(k):
        part = lax.dynamic_index_in_dim(given, at ^ k, 0, keepdims=False)
        return part if k == 0 else lax.ppermute(part, team, [(i, i ^ k) for i in range(members)])

    given = [from_mate(k) for k in range(members)]
    parts = [pltpu.with_memory_space_constraint(part, pltpu.HBM) for part in parts]
    held = pl.pallas_call(
        collect_body,
        out_shape=pltpu.VMEM((2, 2, full, half), bf16),
        in_specs=[pl.BlockSpec(memory_space=pltpu.SMEM)] + [pl.BlockSpec(memory_space=pltpu.HBM)] * len(parts),
        out_specs=vmem,
        scratch_shapes=[pltpu.SemaphoreType.DMA((len(parts),))],
        compiler_params=params,
        name="collect",
    )(jnp.stack([place, core, y_at]), *parts)

    given = jnp.stack([lax.select_n(at ^ k, *given) for k in range(members)]).reshape(2, 2, 2, mine, half)
    slopes, direct_g = (jnp.swapaxes(given[:, :, i], 1, 2).reshape(2, mine, full) for i in (0, 1))

    block = jax.ShapeDtypeStruct((mine, full), bf16)
    tile_of_f32 = jax.ShapeDtypeStruct((8, 128), f32)
    two = jax.ShapeDtypeStruct((2, mine, full), bf16)

    def on_layers(body, out_shape, *arrays, scratch=()):
        return pl.pallas_call(
            body,
            out_shape=out_shape,
            in_specs=[vmem] * (1 + len(arrays)),
            out_specs=jax.tree.map(lambda _: vmem, out_shape),
            scratch_shapes=list(scratch),
            compiler_params=params,
            name=body.__name__,
        )(held, *arrays)

    def product(direct, sums=None):
        room = [pltpu.VMEM((mine, full), bf16)]
        t_1 = on_layers(start_body, block, slopes, direct, scratch=room)
        received = lax.ppermute(t_1, pipe, [(0, 3), (1, 2)])
        t_1, e_0, norm = on_layers(turn_body, (block, block, tile_of_f32), slopes, direct, received, scratch=room)
        received = lax.ppermute(e_0, pipe, [(3, 0), (2, 1)])
        g = on_layers(finish_body, two, slopes, jnp.where(pair == 1, t_1, received))
        norm = jnp.where(pair == 1, norm[:1], 0.0) / total_rows
        g = jnp.swapaxes(g.reshape(2, mine, 2 * z_size, thin), 1, 2)
        g = g.reshape(members * z_size, mine, thin)
        g, norm = lax.optimization_barrier((g, norm))
        if sums is not None:
            g = ride(g, jnp.concatenate([sums, norm]))
        g = lax.all_to_all(g, wide, 0, 0)
        columns = jnp.swapaxes(g[:, :mine].reshape(members, z_size, mine, thin), 0, 1).reshape(z_size * rows, thin)
        parts = matmul(columns.T, hidden_z).astype(bf16).reshape(thin, y_size, tall)
        parts = jnp.swapaxes(parts, 0, 1)
        if sums is not None:
            parts = ride(parts, alight(g, mine))
        parts = lax.all_to_all(parts, "y", 0, 0)
        if sums is not None:
            norm = alight(parts, thin)
        tile = jnp.sum(parts[:, :thin].astype(f32), axis=0) / total_rows
        return tile.astype(bf16), norm

    def ride(array, sums):
        parts = []
        for _ in range(3):
            parts.append(lax.reduce_precision(sums, 8, 7))
            sums = sums - parts[-1]
        parts = jnp.concatenate(parts + [jnp.zeros_like(sums)]).astype(bf16)
        parts = jnp.concatenate([parts] * (array.shape[2] // thin), axis=1)
        return jnp.concatenate([array, jnp.broadcast_to(parts, (array.shape[0], *parts.shape))], axis=1)

    def alight(array, from_row):
        return jnp.sum(array[:, from_row : from_row + 12, :thin].astype(f32).reshape(-1, 4, thin), axis=0)

    u_tile, gu = product(direct_g)
    uu = jnp.sum(u_tile.astype(f32) ** 2)
    row = lax.broadcasted_iota(jnp.int32, (3, thin), 0)
    sums = jnp.where(row == 0, rr0, jnp.where(row == 1, gu, uu))
    u_tile, sums = lax.optimization_barrier((u_tile, sums))
    u_cols = lax.all_to_all(jnp.broadcast_to(u_tile, (y_size, thin, tall)), "y", 0, 0)
    u_cols = jnp.swapaxes(u_cols, 0, 1).reshape(thin, full)
    along = matmul_t(hidden_z, u_cols).astype(bf16).reshape(z_size, members, mine, thin)
    along = jnp.swapaxes(along, 0, 1).reshape(members * z_size, mine, thin)
    along = lax.all_to_all(along, wide, 0, 0).reshape(2, 2 * z_size, mine, thin)
    along = jnp.swapaxes(along, 1, 2).reshape(2, mine, full)
    w_tile, sums = product(along, sums)
    both = jnp.swapaxes(jnp.stack([u_tile, w_tile]), 1, 2).reshape(2, z_size, grad_rows, thin)
    both = lax.all_to_all(both, "z", 1, 1)
    solved, residual = pl.pallas_call(
        update_body,
        out_shape=(jax.ShapeDtypeStruct(grad.shape, f32),) * 2,
        in_specs=[vmem] * 4,
        out_specs=(vmem, vmem),
        compiler_params=params,
        name="update",
    )(sums, swap(sums, "pp"), both, grad)
    return solved[None], residual[None]


def solution(mesh):
    fine = Mesh(mesh.devices.reshape(2, 2, 2, 4, 8), ("pp", "pr", "mp", "y", "z"))
    dp = ("y", "z")
    return jax.shard_map(
        local,
        mesh=fine,
        in_specs=(P(pipe, None, "mp"), P(dp, None), P(dp), P(pipe, dp, "mp")),
        out_specs=(P(pipe, dp, "mp"), P(pipe, dp, "mp")),
        check_vma=False,
    )
```

```python
import functools

import jax
import jax.numpy as jnp
from jax import lax
from jax.experimental import pallas as pl
from jax.experimental.pallas import tpu as pltpu
from jax.sharding import Mesh, PartitionSpec as P

damping = 0.25
bf16 = jnp.bfloat16
f32 = jnp.float32
pipe = ("pp", "pr")
team = ("pr", "mp")
wide = ("pr", "mp", "z")


def matmul(left, right):
    return jnp.dot(left, right, preferred_element_type=f32)


def matmul_t(left, right):
    return lax.dot_general(left, right, (((1,), (1,)), ((), ())), preferred_element_type=f32)


def swap(array, axis):
    return lax.ppermute(array, axis, [(0, 1), (1, 0)])


def shift(array, axis, by):
    size = lax.axis_size(axis)
    return lax.ppermute(array, axis, [(i, (i + by) % size) for i in range(size)])


def shifts(array, axis):
    return [shift(array, axis, k) for k in range(1, lax.axis_size(axis))]


def back(array, w_ref):
    half = w_ref.shape[2]
    return sum(matmul_t(array[:, i * half : (i + 1) * half], w_ref[i]) for i in (0, 1)).astype(bf16)


def pass_layer(array, w_ref, layer, slope_ref, direct_ref, out_ref):
    half = w_ref.shape[2]
    for i in (0, 1):
        at = pl.ds(i * half, half)
        made = matmul(array, w_ref[i]) + direct_ref[layer, :, at].astype(f32)
        out_ref[:, at] = (slope_ref[layer, :, at].astype(f32) * made).astype(bf16)


def load_body(layer, at_ref, *refs):
    parts, (w_ref, sems) = refs[:-2], refs[-2:]
    place, core, y_at = at_ref[0], at_ref[1], at_ref[2]
    count = len(parts) // 2
    chunk = parts[1].shape[0]
    y_size = w_ref.shape[1] // chunk // 2
    own, mate = [], []
    for i, part in enumerate(parts):
        k, column = i % count, core if i < count else 1 - core
        if k == 0:
            own.append(pltpu.make_async_copy(part, w_ref.at[column], sems.at[i]))
        else:
            owner = (y_at + (0, y_size - 1, 1, 2)[(k - 1) // 2]) % y_size
            row = pl.multiple_of((2 * owner + (k - 1) % 2) * chunk, 16)
            mate.append(pltpu.make_async_copy(part, w_ref.at[column, pl.ds(row, chunk)], sems.at[i]))
    for wanted, copies in ((place == layer, own), (place != layer, mate)):

        @pl.when(wanted)
        def _():
            for copy in copies:
                copy.start()
            for copy in copies:
                copy.wait()


def last_body(at_ref, hidden_ref, w_hbm, grad_hbm, out_ref, w_ref, grad_ref, w_sems, grad_sems):
    pair = at_ref[3]
    chunks, z_size = w_sems.shape[0], grad_sems.shape[1]
    step, block = w_ref.shape[0] // chunks, grad_hbm.shape[1]
    w_copies, grad_copies = [], []
    for k in range(chunks):
        at = pl.ds(k * step, step)
        w_copies.append([pltpu.make_async_copy(w_hbm.at[at], w_ref.at[at], w_sems.at[k])])
    for y in range(chunks):
        grad_copies.append([])
        for z in range(z_size):
            to = grad_ref.at[pl.ds((y * z_size + z) * block, block)]
            grad_copies[y].append(pltpu.make_async_copy(grad_hbm.at[z * chunks + y], to, grad_sems.at[y, z]))
    for copies in w_copies + grad_copies:
        for copy in copies:
            copy.start()
    mine = out_ref.shape[2]
    for kind, (held, source) in enumerate(((w_ref, w_copies), (grad_ref, grad_copies))):
        made = None
        for k, copies in enumerate(source):
            for copy in copies:
                copy.wait()
            at = pl.ds(k * step, step)
            more = matmul(hidden_ref[:, at], held[at, :])
            made = more if made is None else made + more
        if kind == 0:
            act = jnp.tanh(made)
            made = 1.0 - act * act
        made = made.astype(bf16)
        for i in range(out_ref.shape[0]):
            out_ref[i ^ (2 * pair), kind] = made[i * mine : (i + 1) * mine]


def begin_body(w_1, slope_ref, direct_ref, t_ref, scratch):
    scratch[...] = (slope_ref[0].astype(f32) * direct_ref[0].astype(f32)).astype(bf16)
    pass_layer(scratch[...], w_1, 1, slope_ref, direct_ref, t_ref)


def turn_body(w_0, w_1, slope_ref, direct_ref, received_ref, t_ref, e_ref, norm_ref, scratch):
    pass_layer(received_ref[...], w_0, 0, slope_ref, direct_ref, scratch)
    pass_layer(scratch[...], w_1, 1, slope_ref, direct_ref, t_ref)
    t_1 = t_ref[...].astype(f32)
    norm_ref[...] = jnp.broadcast_to(jnp.sum(t_1 * t_1, axis=(0, 1), keepdims=True), norm_ref.shape)
    g_1 = (slope_ref[1].astype(f32) * t_1).astype(bf16)
    g_0 = (slope_ref[0].astype(f32) * back(g_1, w_1).astype(f32)).astype(bf16)
    e_ref[...] = back(g_0, w_0)


def finish_body(w_1, slope_ref, e_ref, g_ref):
    g_1 = (slope_ref[1].astype(f32) * e_ref[...].astype(f32)).astype(bf16)
    g_ref[1] = g_1
    g_ref[0] = (slope_ref[0].astype(f32) * back(g_1, w_1).astype(f32)).astype(bf16)


def update_body(sums_ref, other_ref, both_ref, grad_ref, solved_ref, residual_ref):
    thin = sums_ref.shape[1]
    rows = sums_ref[...] + other_ref[...]
    rr0, gu, uu, uw = (rows[i : i + 1] for i in range(4))
    scale = gu + damping * rr0
    len0 = rr0 / scale
    keep = gu / scale
    rr1 = len0 * len0 * (uu - gu * gu / rr0)
    c1 = keep + rr1 / rr0
    c2 = -len0
    d_d = c1 * c1 * rr0 + 2.0 * c1 * c2 * gu + c2 * c2 * uu
    d_image = c1 * c1 * gu + 2.0 * c1 * c2 * uu + c2 * c2 * uw + damping * d_d
    len1 = rr1 / d_image
    for k in range(both_ref.shape[1]):
        at = pl.ds(k * thin, thin)
        g, u, w = grad_ref[:, at], both_ref[0, k].astype(f32), both_ref[1, k].astype(f32)
        direction = c1 * g + c2 * u
        image = c1 * u + c2 * w + damping * direction
        solved_ref[:, at] = len0 * g + len1 * direction
        residual_ref[:, at] = keep * g - len0 * u - len1 * image


vmem = pl.BlockSpec(memory_space=pltpu.VMEM)
params = pltpu.CompilerParams(vmem_limit_bytes=24 << 20)


def local(weights, pool, select, gradient):
    layer_w = weights[0]
    full, half = layer_w.shape
    rows = select.shape[0]
    stages = lax.axis_size(pipe)
    y_size, z_size = lax.axis_size("y"), lax.axis_size("z")
    total_rows = rows * y_size * z_size
    pair, place, core = (lax.axis_index(a) for a in ("pp", "pr", "mp"))
    y_at = lax.axis_index("y")
    stage = 2 * pair + place
    grad = gradient[0]
    grad_rows = grad.shape[0]
    thin = half // z_size
    tall = full // y_size
    members = 4
    mine = rows // members

    chunk = full // y_size // 2
    grad16 = grad.astype(bf16)
    sent = [lax.dynamic_slice_in_dim(layer_w, (2 * y_at + i) * chunk, chunk, 0) for i in (0, 1)]
    grad16, sent[0] = lax.optimization_barrier((grad16, sent[0]))
    a_0, b_0 = (swap(part, "pr") for part in sent)
    own_x = swap(layer_w, "mp")
    others, a_0 = lax.optimization_barrier((shifts(grad16, "y"), a_0))
    others = [grad16] + others
    by_y = jnp.stack([lax.select_n((y_at - k) % y_size, *others) for k in range(y_size)])
    grad_all = lax.all_gather(by_y, "z", axis=0).reshape(y_size * z_size, grad_rows, half)

    first = jnp.take(lax.dynamic_slice_in_dim(pool, core * half, half, 1), select, axis=0)
    first, own_x = lax.optimization_barrier((first, own_x))
    received = first
    for tick in range(stages):
        if tick == 0:
            a_p, a_m = shift(a_0, "y", 1), shift(a_0, "y", -1)
        if tick == 1:
            received, a_p, a_m = lax.optimization_barrier((received, a_p, a_m))
            a_2, b_p, b_m = shift(a_p, "y", 1), shift(b_0, "y", 1), shift(b_0, "y", -1)
            crossed = [swap(part, "mp") for part in (a_0, b_0)]
        if tick == 2:
            received, b_m, crossed, late = lax.optimization_barrier((received, b_m, crossed, grad))
            b_2, rr0 = shift(b_m, "y", -1), jnp.sum(late * late)
            crossed += [swap(part, "mp") for part in (a_p, a_m)]
        if tick == 3:
            received, a_2, b_2, b_p, crossed, rr0 = lax.optimization_barrier((received, a_2, b_2, b_p, crossed, rr0))
            crossed += [swap(part, "mp") for part in (b_p, b_m, a_2, b_2)]
        incoming = first if tick == 0 else jnp.where(stage == 0, first, received)
        hidden = lax.all_gather(incoming, "mp", axis=1, tiled=True)
        if tick + 1 == stages:
            break
        act = jnp.tanh(matmul(hidden, layer_w))
        if tick == 0:
            act, b_0 = lax.optimization_barrier((act, b_0))
        received = lax.ppermute(act.astype(bf16), pipe, [(i, i + 1) for i in range(stages - 1)])

    def in_order(array):
        return jnp.where(pair == 1, jnp.roll(array, rows // 2, axis=0), array)

    hidden_z = lax.all_gather(in_order(hidden), "z", axis=0).reshape(z_size * rows, full)

    position = jnp.stack([place, core, y_at, pair])
    smem, hbm = pl.BlockSpec(memory_space=pltpu.SMEM), pl.BlockSpec(memory_space=pltpu.HBM)
    given = pl.pallas_call(
        last_body,
        out_shape=jax.ShapeDtypeStruct((members, 2, mine, half), bf16),
        in_specs=[smem, vmem, hbm, hbm],
        out_specs=vmem,
        scratch_shapes=[
            pltpu.VMEM((full, half), bf16),
            pltpu.VMEM((full, half), bf16),
            pltpu.SemaphoreType.DMA((y_size,)),
            pltpu.SemaphoreType.DMA((y_size, z_size)),
        ],
        compiler_params=params,
        name="last",
    )(position, hidden, *(pltpu.with_memory_space_constraint(array, pltpu.HBM) for array in (layer_w, grad_all)))
    parts = [layer_w, a_0, b_0, a_p, b_p, a_m, b_m, a_2, b_2, own_x, *(crossed[i] for i in (0, 1, 2, 4, 3, 5, 6, 7))]
    parts, given = lax.optimization_barrier((parts, given))
    at = 2 * place + core

    def from_mate(k):
        part = lax.dynamic_index_in_dim(given, at ^ k, 0, keepdims=False)
        return part if k == 0 else lax.ppermute(part, team, [(i, i ^ k) for i in range(members)])

    given = [from_mate(k) for k in range(members)]
    parts = [pltpu.with_memory_space_constraint(part, pltpu.HBM) for part in parts]
    def load(layer, parts):
        return pl.pallas_call(
            functools.partial(load_body, layer),
            out_shape=pltpu.VMEM((2, full, half), bf16),
            in_specs=[smem] + [hbm] * len(parts),
            out_specs=vmem,
            scratch_shapes=[pltpu.SemaphoreType.DMA((len(parts),))],
            compiler_params=params,
            name=f"load_{layer}",
        )(position, *parts)

    given = jnp.stack([lax.select_n(at ^ k, *given) for k in range(members)]).reshape(2, 2, 2, mine, half)
    slopes, direct_g = (jnp.swapaxes(given[:, :, i], 1, 2).reshape(2, mine, full) for i in (0, 1))

    block = jax.ShapeDtypeStruct((mine, full), bf16)
    tile_of_f32 = jax.ShapeDtypeStruct((8, 128), f32)
    two = jax.ShapeDtypeStruct((2, mine, full), bf16)
    room = pltpu.VMEM((mine, full), bf16)
    def kernel(body, out_shape, *arrays, scratch=()):
        return pl.pallas_call(
            body,
            out_shape=out_shape,
            in_specs=[vmem] * len(arrays),
            out_specs=jax.tree.map(lambda _: vmem, out_shape),
            scratch_shapes=list(scratch),
            compiler_params=params,
            name=body.__name__,
        )(*arrays)

    def product(layers, direct, sums, picks, at_row):
        w_0, w_1 = layers
        t_1 = kernel(begin_body, block, w_1, slopes, direct, scratch=[room])
        received = lax.ppermute(t_1, pipe, [(0, 3), (1, 2)])
        t_1, e_0, norm = kernel(turn_body, (block, block, tile_of_f32), w_0, w_1, slopes, direct, received, scratch=[room])
        received = lax.ppermute(e_0, pipe, [(3, 0), (2, 1)])
        g = kernel(finish_body, two, w_1, slopes, jnp.where(pair == 1, t_1, received))
        sums = sums + picks[at_row] * (jnp.where(pair == 1, norm[:1], 0.0) / total_rows)
        g = jnp.swapaxes(g.reshape(2, mine, 2 * z_size, thin), 1, 2)
        g = g.reshape(members * z_size, mine, thin)
        last = at_row == 3
        g, sums, picks = lax.optimization_barrier((g, sums, picks))
        if last:
            g = ride(g, sums)
        g = lax.all_to_all(g, wide, 0, 0)
        columns = jnp.swapaxes(g[:, :mine].reshape(members, z_size, mine, thin), 0, 1).reshape(z_size * rows, thin)
        parts = matmul(columns.T, hidden_z).astype(bf16).reshape(thin, y_size, tall)
        parts = jnp.swapaxes(parts, 0, 1)
        if last:
            parts = ride(parts, alight(g, mine))
        parts = lax.all_to_all(parts, "y", 0, 0)
        if last:
            sums = alight(parts, thin)
        tile = jnp.sum(parts[:, :thin].astype(f32), axis=0) / total_rows
        return tile.astype(bf16), sums, picks

    def ride(array, sums):
        parts = []
        for _ in range(3):
            parts.append(lax.reduce_precision(sums, 8, 7))
            sums = sums - parts[-1]
        parts = jnp.concatenate(parts + [jnp.zeros_like(sums)]).astype(bf16)
        parts = jnp.concatenate([parts] * (array.shape[2] // thin), axis=1)
        return jnp.concatenate([array, jnp.broadcast_to(parts, (array.shape[0], *parts.shape))], axis=1)

    def alight(array, from_row):
        return jnp.sum(array[:, from_row : from_row + 12, :thin].astype(f32).reshape(-1, 4, thin), axis=0)

    row = lax.broadcasted_iota(jnp.int32, (4, thin), 0)
    picks = [(row == i).astype(f32) for i in range(4)]
    layers = [load(i, parts) for i in (0, 1)]
    u_tile, sums, picks = product(layers, direct_g, picks[0] * rr0, picks, 1)
    uu = jnp.sum(u_tile.astype(f32) ** 2)
    sums = sums + picks[2] * uu
    u_tile, sums, parts = lax.optimization_barrier((u_tile, sums, parts))
    layers = [load(i, parts) for i in (0, 1)]
    others = [u_tile] + shifts(u_tile, "y")
    u_cols = jnp.concatenate([lax.select_n((y_at - k) % y_size, *others) for k in range(y_size)], axis=1)
    along = matmul_t(hidden_z, u_cols).astype(bf16).reshape(z_size, members, mine, thin)
    along = jnp.swapaxes(along, 0, 1).reshape(members * z_size, mine, thin)
    along, layers = lax.optimization_barrier((along, layers))
    along = lax.all_to_all(along, wide, 0, 0).reshape(2, 2 * z_size, mine, thin)
    along = jnp.swapaxes(along, 1, 2).reshape(2, mine, full)
    w_tile, sums, _ = product(layers, along, sums, picks, 3)
    u_tile, w_tile = lax.optimization_barrier((u_tile, w_tile))
    both = jnp.swapaxes(jnp.stack([u_tile, w_tile]), 1, 2).reshape(2, z_size, grad_rows, thin)
    both = lax.all_to_all(both, "z", 1, 1)
    solved, residual = pl.pallas_call(
        update_body,
        out_shape=(jax.ShapeDtypeStruct(grad.shape, f32),) * 2,
        in_specs=[vmem] * 4,
        out_specs=(vmem, vmem),
        compiler_params=params,
        name="update",
    )(sums, swap(sums, "pp"), both, grad)
    return solved[None], residual[None]


def solution(mesh):
    fine = Mesh(mesh.devices.reshape(2, 2, 2, 4, 8), ("pp", "pr", "mp", "y", "z"))
    dp = ("y", "z")
    return jax.shard_map(
        local,
        mesh=fine,
        in_specs=(P(pipe, None, "mp"), P(dp, None), P(dp), P(pipe, dp, "mp")),
        out_specs=(P(pipe, dp, "mp"), P(pipe, dp, "mp")),
        check_vma=False,
    )
```

```python
import functools

import jax
import jax.numpy as jnp
from jax import lax
from jax.experimental import pallas as pl
from jax.experimental.pallas import tpu as pltpu
from jax.sharding import Mesh, PartitionSpec as P

damping = 0.25
bf16 = jnp.bfloat16
f32 = jnp.float32
pipe = ("pp", "pr")
team = ("pr", "mp")
wide = ("pr", "mp", "z")


def matmul(left, right):
    return jnp.dot(left, right, preferred_element_type=f32)


def matmul_t(left, right):
    return lax.dot_general(left, right, (((1,), (1,)), ((), ())), preferred_element_type=f32)


def swap(array, axis):
    return lax.ppermute(array, axis, [(0, 1), (1, 0)])


def shift(array, axis, by):
    size = lax.axis_size(axis)
    return lax.ppermute(array, axis, [(i, (i + by) % size) for i in range(size)])


def shifts(array, axis):
    return [shift(array, axis, k) for k in range(1, lax.axis_size(axis))]


def back(array, w_ref):
    half = w_ref.shape[2]
    return sum(matmul_t(array[:, i * half : (i + 1) * half], w_ref[i]) for i in (0, 1)).astype(bf16)


def pass_layer(array, w_ref, layer, slope_ref, direct_ref, out_ref):
    half = w_ref.shape[2]
    for i in (0, 1):
        at = pl.ds(i * half, half)
        made = matmul(array, w_ref[i]) + direct_ref[layer, :, at].astype(f32)
        out_ref[:, at] = (slope_ref[layer, :, at].astype(f32) * made).astype(bf16)


def load_body(layer, at_ref, *refs):
    parts, (w_ref, sems) = refs[:-2], refs[-2:]
    place, core, y_at = at_ref[0], at_ref[1], at_ref[2]
    count = len(parts) // 2
    chunk = parts[1].shape[0]
    y_size = w_ref.shape[1] // chunk // 2
    own, mate = [], []
    for i, part in enumerate(parts):
        k, column = i % count, core if i < count else 1 - core
        if k == 0:
            own.append(pltpu.make_async_copy(part, w_ref.at[column], sems.at[i]))
        else:
            owner = (y_at + (0, y_size - 1, 1, 2)[(k - 1) // 2]) % y_size
            row = pl.multiple_of((2 * owner + (k - 1) % 2) * chunk, 16)
            mate.append(pltpu.make_async_copy(part, w_ref.at[column, pl.ds(row, chunk)], sems.at[i]))
    for wanted, copies in ((place == layer, own), (place != layer, mate)):

        @pl.when(wanted)
        def _():
            for copy in copies:
                copy.start()
            for copy in copies:
                copy.wait()


def last_body(at_ref, hidden_ref, w_hbm, grad_hbm, out_ref, w_ref, grad_ref, w_sems, grad_sems):
    pair = at_ref[3]
    chunks = w_sems.shape[0]
    step = w_ref.shape[0] // chunks
    w_copies, grad_copies = [], []
    for k in range(chunks):
        at = pl.ds(k * step, step)
        w_copies.append([pltpu.make_async_copy(w_hbm.at[at], w_ref.at[at], w_sems.at[k])])
    for y in range(chunks):
        grad_copies.append([pltpu.make_async_copy(grad_hbm.at[:, y], grad_ref.at[y], grad_sems.at[y])])
    for copies in w_copies + grad_copies:
        for copy in copies:
            copy.start()
    mine = out_ref.shape[2]
    for kind, source in enumerate((w_copies, grad_copies)):
        made = None
        for k, copies in enumerate(source):
            for copy in copies:
                copy.wait()
            at = pl.ds(k * step, step)
            part = grad_ref[k].reshape(step, -1) if kind else w_ref[at, :]
            more = matmul(hidden_ref[:, at], part)
            made = more if made is None else made + more
        if kind == 0:
            act = jnp.tanh(made)
            made = 1.0 - act * act
        made = made.astype(bf16)
        for i in range(out_ref.shape[0]):
            out_ref[i ^ (2 * pair), kind] = made[i * mine : (i + 1) * mine]


def begin_body(w_1, slope_ref, direct_ref, t_ref, scratch):
    scratch[...] = (slope_ref[0].astype(f32) * direct_ref[0].astype(f32)).astype(bf16)
    pass_layer(scratch[...], w_1, 1, slope_ref, direct_ref, t_ref)


def turn_body(w_0, w_1, slope_ref, direct_ref, received_ref, t_ref, e_ref, norm_ref, scratch):
    pass_layer(received_ref[...], w_0, 0, slope_ref, direct_ref, scratch)
    pass_layer(scratch[...], w_1, 1, slope_ref, direct_ref, t_ref)
    t_1 = t_ref[...].astype(f32)
    norm_ref[...] = jnp.broadcast_to(jnp.sum(t_1 * t_1, axis=(0, 1), keepdims=True), norm_ref.shape)
    g_1 = (slope_ref[1].astype(f32) * t_1).astype(bf16)
    g_0 = (slope_ref[0].astype(f32) * back(g_1, w_1).astype(f32)).astype(bf16)
    e_ref[...] = back(g_0, w_0)


def finish_body(w_1, slope_ref, e_ref, g_ref):
    g_1 = (slope_ref[1].astype(f32) * e_ref[...].astype(f32)).astype(bf16)
    g_ref[1] = g_1
    g_ref[0] = (slope_ref[0].astype(f32) * back(g_1, w_1).astype(f32)).astype(bf16)


def update_body(sums_ref, other_ref, both_ref, grad_ref, solved_ref, residual_ref):
    thin = sums_ref.shape[1]
    rows = sums_ref[...] + other_ref[...]
    rr0, gu, uu, uw = (rows[i : i + 1] for i in range(4))
    scale = gu + damping * rr0
    len0 = rr0 / scale
    keep = gu / scale
    rr1 = len0 * len0 * (uu - gu * gu / rr0)
    c1 = keep + rr1 / rr0
    c2 = -len0
    d_d = c1 * c1 * rr0 + 2.0 * c1 * c2 * gu + c2 * c2 * uu
    d_image = c1 * c1 * gu + 2.0 * c1 * c2 * uu + c2 * c2 * uw + damping * d_d
    len1 = rr1 / d_image
    for k in range(both_ref.shape[1]):
        at = pl.ds(k * thin, thin)
        g, u, w = grad_ref[:, at], both_ref[0, k].astype(f32), both_ref[1, k].astype(f32)
        direction = c1 * g + c2 * u
        image = c1 * u + c2 * w + damping * direction
        solved_ref[:, at] = len0 * g + len1 * direction
        residual_ref[:, at] = keep * g - len0 * u - len1 * image


vmem = pl.BlockSpec(memory_space=pltpu.VMEM)
params = pltpu.CompilerParams(vmem_limit_bytes=24 << 20)


def local(weights, pool, select, gradient):
    layer_w = weights[0]
    full, half = layer_w.shape
    rows = select.shape[0]
    stages = lax.axis_size(pipe)
    y_size, z_size = lax.axis_size("y"), lax.axis_size("z")
    total_rows = rows * y_size * z_size
    pair, place, core = (lax.axis_index(a) for a in ("pp", "pr", "mp"))
    y_at = lax.axis_index("y")
    stage = 2 * pair + place
    grad = gradient[0]
    grad_rows = grad.shape[0]
    thin = half // z_size
    tall = full // y_size
    members = 4
    mine = rows // members

    chunk = full // y_size // 2
    grad16 = grad.astype(bf16)
    sent = [lax.dynamic_slice_in_dim(layer_w, (2 * y_at + i) * chunk, chunk, 0) for i in (0, 1)]
    grad16, sent[0] = lax.optimization_barrier((grad16, sent[0]))
    a_0, b_0 = (swap(part, "pr") for part in sent)
    own_x = swap(layer_w, "mp")
    others, a_0 = lax.optimization_barrier((shifts(grad16, "y"), a_0))
    others = [grad16] + others
    by_y = jnp.stack([lax.select_n((y_at - k) % y_size, *others) for k in range(y_size)])
    grad_all = lax.all_gather(by_y, "z", axis=0).reshape(z_size, y_size, grad_rows, half)

    first = jnp.take(lax.dynamic_slice_in_dim(pool, core * half, half, 1), select, axis=0)
    first, own_x = lax.optimization_barrier((first, own_x))
    received = first
    for tick in range(stages):
        if tick == 0:
            a_p, a_m = shift(a_0, "y", 1), shift(a_0, "y", -1)
        if tick == 1:
            received, a_p, a_m = lax.optimization_barrier((received, a_p, a_m))
            a_2, b_p, b_m = shift(a_p, "y", 1), shift(b_0, "y", 1), shift(b_0, "y", -1)
            crossed = [swap(part, "mp") for part in (a_0, b_0)]
        if tick == 2:
            received, b_m, b_p, crossed, late = lax.optimization_barrier((received, b_m, b_p, crossed, grad))
            b_2, rr0 = shift(b_m, "y", -1), jnp.sum(late * late)
            crossed += [swap(part, "mp") for part in (a_p, a_m)]
        if tick == 3:
            received, a_2, b_2, crossed, rr0 = lax.optimization_barrier((received, a_2, b_2, crossed, rr0))
            crossed += [swap(part, "mp") for part in (b_p, b_m, a_2, b_2)]
        incoming = first if tick == 0 else jnp.where(stage == 0, first, received)
        hidden = lax.all_gather(incoming, "mp", axis=1, tiled=True)
        if tick + 1 == stages:
            break
        act = jnp.tanh(matmul(hidden, layer_w))
        if tick == 0:
            act, b_0 = lax.optimization_barrier((act, b_0))
        received = lax.ppermute(act.astype(bf16), pipe, [(i, i + 1) for i in range(stages - 1)])

    def in_order(array):
        return jnp.where(pair == 1, jnp.roll(array, rows // 2, axis=0), array)

    hidden_z = lax.all_gather(in_order(hidden), "z", axis=0).reshape(z_size * rows, full)

    position = jnp.stack([place, core, y_at, pair])
    smem, hbm = pl.BlockSpec(memory_space=pltpu.SMEM), pl.BlockSpec(memory_space=pltpu.HBM)
    given = pl.pallas_call(
        last_body,
        out_shape=jax.ShapeDtypeStruct((members, 2, mine, half), bf16),
        in_specs=[smem, vmem, hbm, hbm],
        out_specs=vmem,
        scratch_shapes=[
            pltpu.VMEM((full, half), bf16),
            pltpu.VMEM((y_size, z_size, grad_rows, half), bf16),
            pltpu.SemaphoreType.DMA((y_size,)),
            pltpu.SemaphoreType.DMA((y_size,)),
        ],
        compiler_params=params,
        name="last",
    )(position, hidden, *(pltpu.with_memory_space_constraint(array, pltpu.HBM) for array in (layer_w, grad_all)))
    parts = [layer_w, a_0, b_0, a_p, b_p, a_m, b_m, a_2, b_2, own_x, *(crossed[i] for i in (0, 1, 2, 4, 3, 5, 6, 7))]
    parts, given = lax.optimization_barrier((parts, given))
    at = 2 * place + core

    def from_mate(k):
        part = lax.dynamic_index_in_dim(given, at ^ k, 0, keepdims=False)
        return part if k == 0 else lax.ppermute(part, team, [(i, i ^ k) for i in range(members)])

    given = [from_mate(k) for k in range(members)]
    parts = [pltpu.with_memory_space_constraint(part, pltpu.HBM) for part in parts]
    def load(layer, parts):
        return pl.pallas_call(
            functools.partial(load_body, layer),
            out_shape=pltpu.VMEM((2, full, half), bf16),
            in_specs=[smem] + [hbm] * len(parts),
            out_specs=vmem,
            scratch_shapes=[pltpu.SemaphoreType.DMA((len(parts),))],
            compiler_params=params,
            name=f"load_{layer}",
        )(position, *parts)

    given = jnp.stack([lax.select_n(at ^ k, *given) for k in range(members)]).reshape(2, 2, 2, mine, half)
    slopes, direct_g = (jnp.swapaxes(given[:, :, i], 1, 2).reshape(2, mine, full) for i in (0, 1))

    block = jax.ShapeDtypeStruct((mine, full), bf16)
    tile_of_f32 = jax.ShapeDtypeStruct((8, 128), f32)
    two = jax.ShapeDtypeStruct((2, mine, full), bf16)
    room = pltpu.VMEM((mine, full), bf16)
    def kernel(body, out_shape, *arrays, scratch=()):
        return pl.pallas_call(
            body,
            out_shape=out_shape,
            in_specs=[vmem] * len(arrays),
            out_specs=jax.tree.map(lambda _: vmem, out_shape),
            scratch_shapes=list(scratch),
            compiler_params=params,
            name=body.__name__,
        )(*arrays)

    def product(layers, direct, sums, picks, at_row):
        w_0, w_1 = layers
        t_1 = kernel(begin_body, block, w_1, slopes, direct, scratch=[room])
        received = lax.ppermute(t_1, pipe, [(0, 3), (1, 2)])
        t_1, e_0, norm = kernel(turn_body, (block, block, tile_of_f32), w_0, w_1, slopes, direct, received, scratch=[room])
        received = lax.ppermute(e_0, pipe, [(3, 0), (2, 1)])
        g = kernel(finish_body, two, w_1, slopes, jnp.where(pair == 1, t_1, received))
        sums = sums + picks[at_row] * (jnp.where(pair == 1, norm[:1], 0.0) / total_rows)
        g = jnp.swapaxes(g.reshape(2, mine, 2 * z_size, thin), 1, 2)
        g = g.reshape(members * z_size, mine, thin)
        last = at_row == 3
        g, sums, picks = lax.optimization_barrier((g, sums, picks))
        if last:
            g = ride(g, sums)
        g = lax.all_to_all(g, wide, 0, 0)
        columns = jnp.swapaxes(g[:, :mine].reshape(members, z_size, mine, thin), 0, 1).reshape(z_size * rows, thin)
        parts = matmul(columns.T, hidden_z).astype(bf16).reshape(thin, y_size, tall)
        parts = jnp.swapaxes(parts, 0, 1)
        if last:
            parts = ride(parts, alight(g, mine))
        parts = lax.all_to_all(parts, "y", 0, 0)
        if last:
            sums = alight(parts, thin)
        tile = jnp.sum(parts[:, :thin].astype(f32), axis=0) / total_rows
        return tile.astype(bf16), sums, picks

    def ride(array, sums):
        parts = []
        for _ in range(3):
            parts.append(lax.reduce_precision(sums, 8, 7))
            sums = sums - parts[-1]
        parts = jnp.concatenate(parts + [jnp.zeros_like(sums)]).astype(bf16)
        parts = jnp.concatenate([parts] * (array.shape[2] // thin), axis=1)
        return jnp.concatenate([array, jnp.broadcast_to(parts, (array.shape[0], *parts.shape))], axis=1)

    def alight(array, from_row):
        return jnp.sum(array[:, from_row : from_row + 12, :thin].astype(f32).reshape(-1, 4, thin), axis=0)

    row = lax.broadcasted_iota(jnp.int32, (4, thin), 0)
    picks = [(row == i).astype(f32) for i in range(4)]
    layers = [load(i, parts) for i in (0, 1)]
    u_tile, sums, picks = product(layers, direct_g, picks[0] * rr0, picks, 1)
    uu = jnp.sum(u_tile.astype(f32) ** 2)
    sums = sums + picks[2] * uu
    u_tile, sums, parts = lax.optimization_barrier((u_tile, sums, parts))
    layers = [load(i, parts) for i in (0, 1)]
    others = [u_tile] + shifts(u_tile, "y")
    u_cols = jnp.concatenate([lax.select_n((y_at - k) % y_size, *others) for k in range(y_size)], axis=1)
    along = matmul_t(hidden_z, u_cols).astype(bf16).reshape(z_size, members, mine, thin)
    along = jnp.swapaxes(along, 0, 1).reshape(members * z_size, mine, thin)
    along, layers = lax.optimization_barrier((along, layers))
    along = lax.all_to_all(along, wide, 0, 0).reshape(2, 2 * z_size, mine, thin)
    along = jnp.swapaxes(along, 1, 2).reshape(2, mine, full)
    w_tile, sums, _ = product(layers, along, sums, picks, 3)
    u_tile, w_tile = lax.optimization_barrier((u_tile, w_tile))
    both = jnp.swapaxes(jnp.stack([u_tile, w_tile]), 1, 2).reshape(2, z_size, grad_rows, thin)
    both = lax.all_to_all(both, "z", 1, 1)
    solved, residual = pl.pallas_call(
        update_body,
        out_shape=(jax.ShapeDtypeStruct(grad.shape, f32),) * 2,
        in_specs=[vmem] * 4,
        out_specs=(vmem, vmem),
        compiler_params=params,
        name="update",
    )(sums, swap(sums, "pp"), both, grad)
    return solved[None], residual[None]


def solution(mesh):
    fine = Mesh(mesh.devices.reshape(2, 2, 2, 4, 8), ("pp", "pr", "mp", "y", "z"))
    dp = ("y", "z")
    return jax.shard_map(
        local,
        mesh=fine,
        in_specs=(P(pipe, None, "mp"), P(dp, None), P(dp), P(pipe, dp, "mp")),
        out_specs=(P(pipe, dp, "mp"), P(pipe, dp, "mp")),
        check_vma=False,
    )
```

```python
import functools

import jax
import jax.numpy as jnp
from jax import lax
from jax.experimental import pallas as pl
from jax.experimental.pallas import tpu as pltpu
from jax.sharding import Mesh, PartitionSpec as P

damping = 0.25
bf16 = jnp.bfloat16
f32 = jnp.float32
pipe = ("pp", "pr")
team = ("pr", "mp")
wide = ("pr", "mp", "z")


def matmul(left, right):
    return jnp.dot(left, right, preferred_element_type=f32)


def matmul_t(left, right):
    return lax.dot_general(left, right, (((1,), (1,)), ((), ())), preferred_element_type=f32)


def swap(array, axis):
    return lax.ppermute(array, axis, [(0, 1), (1, 0)])


def shift(array, axis, by):
    size = lax.axis_size(axis)
    return lax.ppermute(array, axis, [(i, (i + by) % size) for i in range(size)])


def shifts(array, axis):
    return [shift(array, axis, k) for k in range(1, lax.axis_size(axis))]


def back(array, w_ref):
    half = w_ref.shape[2]
    return sum(matmul_t(array[:, i * half : (i + 1) * half], w_ref[i]) for i in (0, 1)).astype(bf16)


def pass_layer(array, w_ref, layer, slope_ref, direct_ref, out_ref):
    half = w_ref.shape[2]
    for i in (0, 1):
        at = pl.ds(i * half, half)
        made = matmul(array, w_ref[i]) + direct_ref[layer, :, at].astype(f32)
        out_ref[:, at] = (slope_ref[layer, :, at].astype(f32) * made).astype(bf16)


def load_body(layer, at_ref, *refs):
    parts, (w_ref, sems) = refs[:-2], refs[-2:]
    place, core, y_at = at_ref[0], at_ref[1], at_ref[2]
    count = len(parts) // 2
    chunk = parts[1].shape[0]
    y_size = w_ref.shape[1] // chunk // 2
    own, mate = [], []
    for i, part in enumerate(parts):
        k, column = i % count, core if i < count else 1 - core
        if k == 0:
            own.append(pltpu.make_async_copy(part, w_ref.at[column], sems.at[i]))
        else:
            owner = (y_at + (0, y_size - 1, 1, 2)[(k - 1) // 2]) % y_size
            row = pl.multiple_of((2 * owner + (k - 1) % 2) * chunk, 16)
            mate.append(pltpu.make_async_copy(part, w_ref.at[column, pl.ds(row, chunk)], sems.at[i]))
    for wanted, copies in ((place == layer, own), (place != layer, mate)):

        @pl.when(wanted)
        def _():
            for copy in copies:
                copy.start()
            for copy in copies:
                copy.wait()


def last_body(at_ref, hidden_ref, w_hbm, grad_hbm, out_ref, w_ref, grad_ref, w_sems, grad_sems):
    pair = at_ref[3]
    chunks = w_sems.shape[0]
    step = w_ref.shape[0] // chunks
    w_copies, grad_copies = [], []
    for k in range(chunks):
        at = pl.ds(k * step, step)
        w_copies.append([pltpu.make_async_copy(w_hbm.at[at], w_ref.at[at], w_sems.at[k])])
    for y in range(chunks):
        grad_copies.append([pltpu.make_async_copy(grad_hbm.at[:, y], grad_ref.at[y], grad_sems.at[y])])
    for copies in w_copies + grad_copies:
        for copy in copies:
            copy.start()
    mine = out_ref.shape[2]
    for kind, source in enumerate((w_copies, grad_copies)):
        made = None
        for k, copies in enumerate(source):
            for copy in copies:
                copy.wait()
            at = pl.ds(k * step, step)
            part = grad_ref[k].reshape(step, -1) if kind else w_ref[at, :]
            more = matmul(hidden_ref[:, at], part)
            made = more if made is None else made + more
        if kind == 0:
            act = jnp.tanh(made)
            made = 1.0 - act * act
        made = made.astype(bf16)
        for i in range(out_ref.shape[0]):
            out_ref[i ^ (2 * pair), kind] = made[i * mine : (i + 1) * mine]


def begin_body(w_1, slope_ref, direct_ref, t_ref, scratch):
    scratch[...] = (slope_ref[0].astype(f32) * direct_ref[0].astype(f32)).astype(bf16)
    pass_layer(scratch[...], w_1, 1, slope_ref, direct_ref, t_ref)


def turn_body(w_0, w_1, slope_ref, direct_ref, received_ref, t_ref, e_ref, norm_ref, scratch):
    pass_layer(received_ref[...], w_0, 0, slope_ref, direct_ref, scratch)
    pass_layer(scratch[...], w_1, 1, slope_ref, direct_ref, t_ref)
    t_1 = t_ref[...].astype(f32)
    norm_ref[...] = jnp.broadcast_to(jnp.sum(t_1 * t_1, axis=(0, 1), keepdims=True), norm_ref.shape)
    g_1 = (slope_ref[1].astype(f32) * t_1).astype(bf16)
    g_0 = (slope_ref[0].astype(f32) * back(g_1, w_1).astype(f32)).astype(bf16)
    e_ref[...] = back(g_0, w_0)


def finish_body(w_1, slope_ref, e_ref, g_ref):
    g_1 = (slope_ref[1].astype(f32) * e_ref[...].astype(f32)).astype(bf16)
    g_ref[1] = g_1
    g_ref[0] = (slope_ref[0].astype(f32) * back(g_1, w_1).astype(f32)).astype(bf16)


def update_body(sums_ref, other_ref, both_ref, grad_ref, solved_ref, residual_ref):
    thin = sums_ref.shape[1]
    rows = sums_ref[...] + other_ref[...]
    rr0, gu, uu, uw = (rows[i : i + 1] for i in range(4))
    scale = gu + damping * rr0
    len0 = rr0 / scale
    keep = gu / scale
    rr1 = len0 * len0 * (uu - gu * gu / rr0)
    c1 = keep + rr1 / rr0
    c2 = -len0
    d_d = c1 * c1 * rr0 + 2.0 * c1 * c2 * gu + c2 * c2 * uu
    d_image = c1 * c1 * gu + 2.0 * c1 * c2 * uu + c2 * c2 * uw + damping * d_d
    len1 = rr1 / d_image
    for k in range(both_ref.shape[1]):
        at = pl.ds(k * thin, thin)
        g, u, w = grad_ref[:, at], both_ref[0, k].astype(f32), both_ref[1, k].astype(f32)
        direction = c1 * g + c2 * u
        image = c1 * u + c2 * w + damping * direction
        solved_ref[:, at] = len0 * g + len1 * direction
        residual_ref[:, at] = keep * g - len0 * u - len1 * image


vmem = pl.BlockSpec(memory_space=pltpu.VMEM)
params = pltpu.CompilerParams(vmem_limit_bytes=24 << 20)


def local(weights, pool, select, gradient):
    layer_w = weights[0]
    full, half = layer_w.shape
    rows = select.shape[0]
    stages = lax.axis_size(pipe)
    y_size, z_size = lax.axis_size("y"), lax.axis_size("z")
    total_rows = rows * y_size * z_size
    pair, place, core = (lax.axis_index(a) for a in ("pp", "pr", "mp"))
    y_at = lax.axis_index("y")
    stage = 2 * pair + place
    grad = gradient[0]
    grad_rows = grad.shape[0]
    thin = half // z_size
    tall = full // y_size
    members = 4
    mine = rows // members

    chunk = full // y_size // 2
    grad16 = grad.astype(bf16)
    sent = [lax.dynamic_slice_in_dim(layer_w, (2 * y_at + i) * chunk, chunk, 0) for i in (0, 1)]
    grad16, sent[0] = lax.optimization_barrier((grad16, sent[0]))
    a_0, b_0 = (swap(part, "pr") for part in sent)
    own_x = swap(layer_w, "mp")
    others, a_0 = lax.optimization_barrier((shifts(grad16, "y"), a_0))
    others = [grad16] + others
    by_y = jnp.stack([lax.select_n((y_at - k) % y_size, *others) for k in range(y_size)])
    grad_all = lax.all_gather(by_y, "z", axis=0).reshape(z_size, y_size, grad_rows, half)

    first = jnp.take(lax.dynamic_slice_in_dim(pool, core * half, half, 1), select, axis=0)
    first, own_x = lax.optimization_barrier((first, own_x))
    received = first
    for tick in range(stages):
        if tick == 0:
            a_p, a_m = shift(a_0, "y", 1), shift(a_0, "y", -1)
        if tick == 1:
            received, a_p, a_m = lax.optimization_barrier((received, a_p, a_m))
            a_2, b_p, b_m = shift(a_p, "y", 1), shift(b_0, "y", 1), shift(b_0, "y", -1)
            crossed = [swap(part, "mp") for part in (a_0, b_0)]
        if tick == 2:
            received, b_m, b_p, crossed, late = lax.optimization_barrier((received, b_m, b_p, crossed, grad))
            b_2, rr0 = shift(b_m, "y", -1), jnp.sum(late * late)
            crossed += [swap(part, "mp") for part in (a_p, a_m)]
        if tick == 3:
            received, a_2, b_2, crossed, rr0 = lax.optimization_barrier((received, a_2, b_2, crossed, rr0))
            crossed += [swap(part, "mp") for part in (b_p, b_m, a_2, b_2)]
        incoming = first if tick == 0 else jnp.where(stage == 0, first, received)
        hidden = lax.all_gather(incoming, "mp", axis=1, tiled=True)
        if tick + 1 == stages:
            break
        act = jnp.tanh(matmul(hidden, layer_w))
        if tick == 0:
            act, b_0 = lax.optimization_barrier((act, b_0))
        received = lax.ppermute(act.astype(bf16), pipe, [(i, i + 1) for i in range(stages - 1)])

    def in_order(array):
        return jnp.where(pair == 1, jnp.roll(array, rows // 2, axis=0), array)

    hidden_z = lax.all_gather(in_order(hidden), "z", axis=0).reshape(z_size * rows, full)

    position = jnp.stack([place, core, y_at, pair])
    smem, hbm = pl.BlockSpec(memory_space=pltpu.SMEM), pl.BlockSpec(memory_space=pltpu.HBM)
    given = pl.pallas_call(
        last_body,
        out_shape=jax.ShapeDtypeStruct((members, 2, mine, half), bf16),
        in_specs=[smem, vmem, hbm, hbm],
        out_specs=vmem,
        scratch_shapes=[
            pltpu.VMEM((full, half), bf16),
            pltpu.VMEM((y_size, z_size, grad_rows, half), bf16),
            pltpu.SemaphoreType.DMA((y_size,)),
            pltpu.SemaphoreType.DMA((y_size,)),
        ],
        compiler_params=params,
        name="last",
    )(position, hidden, *(pltpu.with_memory_space_constraint(array, pltpu.HBM) for array in (layer_w, grad_all)))
    parts = [layer_w, a_0, b_0, a_p, b_p, a_m, b_m, a_2, b_2, own_x, *(crossed[i] for i in (0, 1, 2, 4, 3, 5, 6, 7))]
    parts, given = lax.optimization_barrier((parts, given))
    at = 2 * place + core

    def from_mate(k):
        part = lax.dynamic_index_in_dim(given, at ^ k, 0, keepdims=False)
        return part if k == 0 else lax.ppermute(part, team, [(i, i ^ k) for i in range(members)])

    given = [from_mate(k) for k in range(members)]
    parts = [pltpu.with_memory_space_constraint(part, pltpu.HBM) for part in parts]
    def load(layer, parts):
        return pl.pallas_call(
            functools.partial(load_body, layer),
            out_shape=pltpu.VMEM((2, full, half), bf16),
            in_specs=[smem] + [hbm] * len(parts),
            out_specs=vmem,
            scratch_shapes=[pltpu.SemaphoreType.DMA((len(parts),))],
            compiler_params=params,
            name=f"load_{layer}",
        )(position, *parts)

    layers = [load(i, parts) for i in (0, 1)]
    given, layers = lax.optimization_barrier((given, layers))
    given = jnp.stack([lax.select_n(at ^ k, *given) for k in range(members)]).reshape(2, 2, 2, mine, half)
    slopes, direct_g = (jnp.swapaxes(given[:, :, i], 1, 2).reshape(2, mine, full) for i in (0, 1))

    block = jax.ShapeDtypeStruct((mine, full), bf16)
    tile_of_f32 = jax.ShapeDtypeStruct((8, 128), f32)
    two = jax.ShapeDtypeStruct((2, mine, full), bf16)
    room = pltpu.VMEM((mine, full), bf16)
    def kernel(body, out_shape, *arrays, scratch=()):
        return pl.pallas_call(
            body,
            out_shape=out_shape,
            in_specs=[vmem] * len(arrays),
            out_specs=jax.tree.map(lambda _: vmem, out_shape),
            scratch_shapes=list(scratch),
            compiler_params=params,
            name=body.__name__,
        )(*arrays)

    def product(layers, direct, sums, picks, at_row):
        w_0, w_1 = layers
        t_1 = kernel(begin_body, block, w_1, slopes, direct, scratch=[room])
        received = lax.ppermute(t_1, pipe, [(0, 3), (1, 2)])
        t_1, e_0, norm = kernel(turn_body, (block, block, tile_of_f32), w_0, w_1, slopes, direct, received, scratch=[room])
        received = lax.ppermute(e_0, pipe, [(3, 0), (2, 1)])
        g = kernel(finish_body, two, w_1, slopes, jnp.where(pair == 1, t_1, received))
        sums = sums + picks[at_row] * (jnp.where(pair == 1, norm[:1], 0.0) / total_rows)
        g = jnp.swapaxes(g.reshape(2, mine, 2 * z_size, thin), 1, 2)
        g = g.reshape(members * z_size, mine, thin)
        last = at_row == 3
        g, sums, picks = lax.optimization_barrier((g, sums, picks))
        if last:
            g = ride(g, sums)
        g = lax.all_to_all(g, wide, 0, 0)
        columns = jnp.swapaxes(g[:, :mine].reshape(members, z_size, mine, thin), 0, 1).reshape(z_size * rows, thin)
        parts = matmul(columns.T, hidden_z).astype(bf16).reshape(thin, y_size, tall)
        parts = jnp.swapaxes(parts, 0, 1)
        if last:
            parts = ride(parts, alight(g, mine))
        parts = lax.all_to_all(parts, "y", 0, 0)
        if last:
            sums = alight(parts, thin)
        tile = jnp.sum(parts[:, :thin].astype(f32), axis=0) / total_rows
        return tile.astype(bf16), sums, picks

    def ride(array, sums):
        parts = []
        for _ in range(3):
            parts.append(lax.reduce_precision(sums, 8, 7))
            sums = sums - parts[-1]
        parts = jnp.concatenate(parts + [jnp.zeros_like(sums)]).astype(bf16)
        parts = jnp.concatenate([parts] * (array.shape[2] // thin), axis=1)
        return jnp.concatenate([array, jnp.broadcast_to(parts, (array.shape[0], *parts.shape))], axis=1)

    def alight(array, from_row):
        return jnp.sum(array[:, from_row : from_row + 12, :thin].astype(f32).reshape(-1, 4, thin), axis=0)

    row = lax.broadcasted_iota(jnp.int32, (4, thin), 0)
    picks = [(row == i).astype(f32) for i in range(4)]
    u_tile, sums, picks = product(layers, direct_g, picks[0] * rr0, picks, 1)
    uu = jnp.sum(u_tile.astype(f32) ** 2)
    sums = sums + picks[2] * uu
    u_tile, sums, parts = lax.optimization_barrier((u_tile, sums, parts))
    layers = [load(i, parts) for i in (0, 1)]
    others = [u_tile] + shifts(u_tile, "y")
    u_cols = jnp.concatenate([lax.select_n((y_at - k) % y_size, *others) for k in range(y_size)], axis=1)
    along = matmul_t(hidden_z, u_cols).astype(bf16).reshape(z_size, members, mine, thin)
    along = jnp.swapaxes(along, 0, 1).reshape(members * z_size, mine, thin)
    along, layers = lax.optimization_barrier((along, layers))
    along = lax.all_to_all(along, wide, 0, 0).reshape(2, 2 * z_size, mine, thin)
    along = jnp.swapaxes(along, 1, 2).reshape(2, mine, full)
    w_tile, sums, _ = product(layers, along, sums, picks, 3)
    u_tile, w_tile = lax.optimization_barrier((u_tile, w_tile))
    both = jnp.swapaxes(jnp.stack([u_tile, w_tile]), 1, 2).reshape(2, z_size, grad_rows, thin)
    both = lax.all_to_all(both, "z", 1, 1)
    solved, residual = pl.pallas_call(
        update_body,
        out_shape=(jax.ShapeDtypeStruct(grad.shape, f32),) * 2,
        in_specs=[vmem] * 4,
        out_specs=(vmem, vmem),
        compiler_params=params,
        name="update",
    )(sums, swap(sums, "pp"), both, grad)
    return solved[None], residual[None]


def solution(mesh):
    fine = Mesh(mesh.devices.reshape(2, 2, 2, 4, 8), ("pp", "pr", "mp", "y", "z"))
    dp = ("y", "z")
    return jax.shard_map(
        local,
        mesh=fine,
        in_specs=(P(pipe, None, "mp"), P(dp, None), P(dp), P(pipe, dp, "mp")),
        out_specs=(P(pipe, dp, "mp"), P(pipe, dp, "mp")),
        check_vma=False,
    )
```
